256 devices in a mesh: row: 16 (over x_lo, z), col: 16 (over x_hi, y, core).
Axes of the slice: x: 4 (x_hi: 2, x_lo: 2; x = x_hi * 2 + x_lo), y: 4, z: 8, core: 2. Of those that a mesh axis runs over, the one named last changes fastest.
Arguments:
- hidden_in: bfloat16 [12288, 5120], P('row', 'col'), may hold values from -6 to 6
- modulation: bfloat16 [48, 3, 5120], P(None, None, 'col'), may hold values from -3 to 3
- w_qkv: bfloat16 [5120, 12288], P('row', 'col'), may hold values from -0.078125 to 0.078125
- w_out: bfloat16 [4096, 5120], P('row', 'col'), may hold values from -0.09375 to 0.09375
- prefix_cache: bfloat16 [16, 256, 8192], P('row', None, 'col'), may hold values from -48 to 48
- req_group: int32 [48], replicated, may hold values from 0 to 3
- req_len: int32 [48], replicated, may hold values from 1 to 672, 12288 in all
- owner: int32 [4], replicated, may hold values from 0 to 15, as said below
Outputs:
- hidden_out: bfloat16 [12288, 5120], P('row', 'col')
- suffix_keys: bfloat16 [12288, 4096], P('row', 'col')
- suffix_values: bfloat16 [12288, 4096], P('row', 'col')
The draws below stay inside these ranges and needn't reach their ends.
Inputs may be any that keep to these rules, and one draw needn't show every extreme that they name: `owner`: the 4 slots are distinct; slot 0 and slot 16 - 1 always hold a group.
All inputs are finite; a program needn't handle non-finite values.
Results may differ from the reference program's by a relative error of at most 0.006.
Values may be sent and summed in bfloat16 or wider, within the bound.
A program may use at most 192 MiB of HBM per device.

```python
import math
import jax
import jax.numpy as jnp
import numpy as np
from jax import lax

D = 5120
HEADS = 32
HD = 128
TOK_DEV = 768
PREFIX = 256
GROUPS = 4
REQS = 48
TOKENS = 12288
MOST_LEN = 672
N_ROW = 16


def draw_owner(key, part):
    middle = jax.random.permutation(key, jnp.arange(1, N_ROW - 1, dtype=jnp.int32))
    chosen = jnp.concatenate([jnp.array([0, N_ROW - 1], dtype=jnp.int32), middle[:GROUPS - 2]])
    return jax.random.permutation(jax.random.fold_in(key, 7), chosen).astype(jnp.int32)


def draw_prefix_cache(key, part):
    key_base = jax.random.fold_in(key, 11)
    layout = (N_ROW, PREFIX, HEADS, 2, HD)
    cache = jax.random.truncated_normal(key_base, -6.0, 6.0, layout, jnp.float32)
    return cache.reshape(N_ROW, PREFIX, 2 * HEADS * HD).astype(jnp.bfloat16)


def place_ends(values, rng, low, top_value):
    spot = [jax.random.randint(jax.random.fold_in(rng, axis), (), 0, length) for axis, length in enumerate(values.shape)]
    longest = values.shape.index(max(values.shape))
    neighbour = spot[:longest] + [(spot[longest] + 1) % values.shape[longest]] + spot[longest + 1:]
    return values.at[tuple(spot)].set(low).at[tuple(neighbour)].set(top_value)


def shard_levels(stream_key, shape, pieces, low, high):
    level, own = 1.0, jax.random.fold_in(stream_key, 6)
    for dim, blocks in pieces:
        heights = jnp.exp(jax.random.uniform(jax.random.fold_in(own, dim), (blocks,), jnp.float32, low / len(pieces), high / len(pieces)))
        level = level * jnp.repeat(heights, shape[dim] // blocks).reshape([-1 if axis == dim else 1 for axis in range(len(shape))])
    return level


def profile(number_of, total, reach, skew):
    weights = [(1 << 20) // math.isqrt(standing ** skew) + 1 for standing in range(2, number_of + 1)]
    surplus, given = total - reach - (number_of - 1), [1] * (number_of - 1)
    while surplus > 0:
        movable = [i for i in range(number_of - 1) if given[i] < reach]
        pool, budget = sum([weights[i] for i in movable]), surplus
        for i in movable:
            extra = min(reach - given[i], max(1, budget * weights[i] // pool), surplus)
            given[i] = given[i] + extra
            surplus = surplus - extra
    return np.array([reach] + given)


def ragged_sizes(own_key, number_of, total, bound, slope):
    if number_of == 2:
        one = jax.random.randint(own_key, (), max(1, total - bound), min(bound, total - 1) + 1)
        return jnp.stack([one, total - one])
    sizes = jnp.asarray(profile(number_of, total, bound, slope), jnp.int32)
    couples = (number_of - 1) // 2
    donor, taker = sizes[1:1 + 2 * couples:2], sizes[2:2 + 2 * couples:2]
    slack = jnp.minimum(donor - 1, bound - taker)
    shifted = jax.random.randint(jax.random.fold_in(own_key, 1), (couples,), 0, 1 << 20) % (slack + 1)
    sizes = sizes.at[1:1 + 2 * couples:2].set(donor - shifted).at[2:2 + 2 * couples:2].set(taker + shifted)
    return sizes[jax.random.permutation(jax.random.fold_in(own_key, 2), number_of)]


def gaussian(own_key, dims, spread, most, pieces=(), held_as=jnp.bfloat16):
    entries = jax.random.normal(own_key, dims, jnp.float32) * spread
    if len(pieces) > 0:
        entries = shard_levels(own_key, dims, pieces, -0.22, 0.18) * entries
    return jnp.clip(entries, min=-most, max=most).astype(held_as)


def setup_inputs(seed: int = 0) -> dict:
    splits = jax.random.split(jax.random.key(seed), 9)
    return {
        "hidden_in": gaussian(splits[0], (TOKENS, D), 1.0, 6.0, ((0, 16), (1, 16))),
        "modulation": gaussian(splits[1], (REQS, 3, D), 0.5, 3.0, ((2, 16),)),
        "w_qkv": gaussian(splits[2], (D, 3 * HEADS * HD), D ** -0.5, 0.078125, ((0, 16), (1, 16))),
        "w_out": gaussian(splits[3], (HEADS * HD, D), (HEADS * HD) ** -0.5, 0.09375, ((0, 16), (1, 16))),
        "prefix_cache": draw_prefix_cache(jax.random.fold_in(splits[8], 71), 0),
        "req_group": place_ends(jax.random.randint(splits[5], (REQS,), 0, GROUPS), jax.random.fold_in(splits[5], 1), 0, GROUPS - 1).astype(jnp.int32),
        "req_len": ragged_sizes(splits[6], REQS, TOKENS, MOST_LEN, 2).astype(jnp.int32),
        "owner": draw_owner(jax.random.fold_in(splits[8], 71), 0),
    }


def request_of(positions, req_len):
    starts = (jnp.cumsum(req_len) - req_len).astype(jnp.int32)
    inside = (starts[None, :] <= positions[:, None]).astype(jnp.int32)
    return (lax.optimization_barrier(jnp.sum(inside, axis=1)) - 1).astype(jnp.int32)

def reference(hidden_in, modulation, w_qkv, w_out, prefix_cache, req_group, req_len, owner):
    positions = jnp.arange(TOKENS, dtype=jnp.int32)
    request_id = request_of(positions, req_len)
    onehot = (request_id[:, None] == jnp.arange(REQS, dtype=jnp.int32)[None, :]).astype(jnp.bfloat16)
    per_token = jnp.dot(onehot, modulation.reshape(REQS, 3 * D), preferred_element_type=jnp.float32)
    shift_rows = per_token[:, :D]
    scale_rows = per_token[:, D:2 * D]
    gate_rows = per_token[:, 2 * D:]
    hidden_f = hidden_in.astype(jnp.float32)
    average = lax.optimization_barrier(jnp.mean(hidden_f, axis=1, keepdims=True))
    centred = hidden_f - average
    variance = lax.optimization_barrier(jnp.mean(centred * centred, axis=1, keepdims=True))
    modulated = (centred * lax.rsqrt(variance + 1e-06) * (1.0 + scale_rows) + shift_rows).astype(jnp.bfloat16)
    projected_qkv = jnp.dot(modulated, w_qkv, preferred_element_type=jnp.float32).astype(jnp.bfloat16)
    projected_qkv = projected_qkv.reshape(TOKENS, HEADS, 3, HD)
    queries = projected_qkv[:, :, 0]
    new_keys = projected_qkv[:, :, 1]
    new_values = projected_qkv[:, :, 2]
    token_group = req_group[request_id].astype(jnp.int32)
    slots = prefix_cache.reshape(N_ROW, PREFIX, HEADS, 2, HD)[owner]
    prefix_keys = slots[:, :, :, 0].reshape(GROUPS * PREFIX, HEADS, HD).astype(jnp.float32)
    prefix_values = slots[:, :, :, 1].reshape(GROUPS * PREFIX, HEADS, HD).astype(jnp.float32)
    prefix_group = jnp.repeat(jnp.arange(GROUPS, dtype=jnp.int32), PREFIX)
    zero_block = jnp.zeros((TOK_DEV, HEADS, HD), jnp.bfloat16)
    keys_padded = jnp.concatenate([zero_block, new_keys, zero_block], axis=0)
    values_padded = jnp.concatenate([zero_block, new_values, zero_block], axis=0)
    outside = jnp.full((TOK_DEV,), -1, jnp.int32)
    request_padded = jnp.concatenate([outside, request_id, outside], axis=0)
    factor = 1.0 / math.sqrt(HD)

    def block(index):
        first = (index * TOK_DEV).astype(jnp.int32)
        query_block = lax.dynamic_slice_in_dim(queries, first, TOK_DEV, 0).astype(jnp.float32)
        query_req = lax.dynamic_slice_in_dim(request_id, first, TOK_DEV, 0)
        query_grp = lax.dynamic_slice_in_dim(token_group, first, TOK_DEV, 0)
        near_keys = lax.dynamic_slice_in_dim(keys_padded, first, 3 * TOK_DEV, 0).astype(jnp.float32)
        near_values = lax.dynamic_slice_in_dim(values_padded, first, 3 * TOK_DEV, 0).astype(jnp.float32)
        key_req = lax.dynamic_slice_in_dim(request_padded, first, 3 * TOK_DEV, 0)
        near_mask = key_req[None, :] == query_req[:, None]
        prefix_mask = prefix_group[None, :] == query_grp[:, None]
        all_keys = jnp.concatenate([prefix_keys, near_keys], axis=0)
        all_values = jnp.concatenate([prefix_values, near_values], axis=0)
        all_mask = jnp.concatenate([prefix_mask, near_mask], axis=1)[:, None, :]
        scores = jnp.einsum('thd,khd->thk', query_block, all_keys) * factor
        scores = jnp.where(all_mask, scores, -1e+30)
        largest = lax.optimization_barrier(jnp.max(scores, axis=2, keepdims=True))
        weights = jnp.where(all_mask, jnp.exp(scores - largest), 0.0)
        denominator = lax.optimization_barrier(jnp.sum(weights, axis=2))
        rounded = lax.optimization_barrier(weights.astype(jnp.bfloat16)).astype(jnp.float32)
        summed = jnp.einsum('thk,khd->thd', rounded, all_values)
        return (summed / denominator[:, :, None]).astype(jnp.bfloat16).reshape(TOK_DEV, HEADS * HD)
    attended = lax.map(block, jnp.arange(N_ROW, dtype=jnp.int32)).reshape(TOKENS, HEADS * HD)
    projected = jnp.dot(attended, w_out, preferred_element_type=jnp.float32)
    hidden_out = (hidden_f + gate_rows * projected).astype(jnp.bfloat16)
    return (hidden_out, new_keys.reshape(TOKENS, HEADS * HD), new_values.reshape(TOKENS, HEADS * HD))
```

```python
import functools
import math

import jax
import jax.numpy as jnp
from jax import lax
from jax.experimental import pallas as pl
from jax.experimental.pallas import tpu as pltpu
from jax.sharding import PartitionSpec as P

HD = 128
N_Z = 8
N_Y = 4
MESH = pl.DeviceIdType.MESH
BIG = 1e30
VMEM_LIMIT = 56 << 20


def contract_first(a, b):
    return lax.dot_general(a, b, (((0,), (0,)), ((), ())), preferred_element_type=jnp.float32)


class Place:
    def __init__(self):
        self.row, self.col = lax.axis_index("row"), lax.axis_index("col")
        self.l, self.z = self.row // N_Z, self.row % N_Z
        self.h, self.y, self.k = self.col // (2 * N_Y), (self.col // 2) % N_Y, self.col % 2

    def row_at(self, plane, dz):
        l = 1 - self.l if plane else self.l
        return l * N_Z + (self.z + dz + N_Z) % N_Z

    def col_at(self, half, dy, core):
        h = 1 - self.h if half else self.h
        k = 1 - self.k if core else self.k
        return (h * N_Y + (self.y + dy + N_Y) % N_Y) * 2 + k

    def z_dev(self, dz):
        return (self.row_at(0, dz), self.col)

    def x_dev(self):
        return (self.row_at(1, 0), self.col)

    def y_dev(self, dy):
        return (self.row, self.col_at(0, dy, 0))

    def half_dev(self):
        return (self.row, self.col_at(1, 0, 0))

    def core_dev(self):
        return (self.row, self.col_at(0, 0, 1))

    def col_dev(self, offset):
        return (self.row, (self.col + offset) % 16)


class Wire:
    def __init__(self, send_sem, recv_sem):
        self.send_sem, self.recv_sem = send_sem, recv_sem
        self.index, self.sent = {}, []

    def slot(self, name):
        return self.index.setdefault(name, len(self.index))

    def copy(self, name, src, dst, dev):
        n = self.slot(name)
        return pltpu.make_async_remote_copy(
            src_ref=src,
            dst_ref=dst,
            send_sem=self.send_sem.at[n],
            recv_sem=self.recv_sem.at[n],
            device_id=dev,
            device_id_type=MESH,
        )

    def send(self, name, src, dst, dev):
        c = self.copy(name, src, dst, dev)
        c.start()
        self.sent.append(c)

    def arrived(self, name, landed, dev):
        self.copy(name, landed, landed, dev).wait_recv()

    def drain(self):
        for c in self.sent:
            c.wait_send()


def meet(devices):
    barrier = pltpu.get_barrier_semaphore()
    for dev in devices:
        pl.semaphore_signal(barrier, inc=1, device_id=dev, device_id_type=MESH)
    pl.semaphore_wait(barrier, len(devices))


class ColGather:
    def __init__(self, at, wire, part):
        self.at, self.wire, self.part = at, wire, part

    def peers(self):
        at = self.at
        return [at.y_dev(1), at.y_dev(-1), at.half_dev(), at.core_dev()]

    def push(self, name, col, piece, dev):
        self.wire.send(name, self.part(col, piece), self.part(col, piece), dev)

    def start(self):
        at = self.at
        self.push(("half",), at.col, None, at.half_dev())
        for d in (1, -1):
            self.push(("y", d, 1, 0), at.col, None, at.y_dev(d))
        self.push(("core", 0, 0, None), at.col, None, at.core_dev())

    def halves(self):
        at = self.at
        block = at.col_at(1, 0, 0)
        self.wire.arrived(("half",), self.part(block, None), at.half_dev())
        for d in (1, -1):
            self.push(("y", d, 1, 1), block, None, at.y_dev(d))
        self.push(("core", 1, 0, None), block, None, at.core_dev())

    def first(self, kind):
        at = self.at
        for d in (1, -1):
            block = at.col_at(kind, -d, 0)
            self.wire.arrived(("y", d, 1, kind), self.part(block, None), at.y_dev(-d))
            piece = 0 if d == 1 else 1
            self.push(("y", d, 2, kind), block, piece, at.y_dev(d))
            self.push(("core", kind, -d, None), block, None, at.core_dev())

    def second(self, kind):
        at = self.at
        for d in (1, -1):
            piece = 0 if d == 1 else 1
            block = at.col_at(kind, 2, 0)
            self.wire.arrived(("y", d, 2, kind), self.part(block, piece), at.y_dev(-d))
            self.push(("core", kind, 2, piece), block, piece, at.core_dev())

    def from_core(self):
        at = self.at
        for kind in (0, 1):
            for dy, piece in ((0, None), (-1, None), (1, None), (2, 0), (2, 1)):
                block = at.col_at(kind, dy, 1)
                self.wire.arrived(("core", kind, dy, piece), self.part(block, piece), at.core_dev())


class RowGather:
    def __init__(self, at, wire, part):
        self.at, self.wire, self.part = at, wire, part

    def peers(self):
        at = self.at
        return [at.z_dev(1), at.z_dev(-1), at.x_dev()]

    def push(self, name, row, half, piece, dev):
        self.wire.send(name, self.part(row, half, piece), self.part(row, half, piece), dev)

    def start(self):
        at = self.at
        self.push(("xa",), at.row, 0, None, at.x_dev())
        for d in (1, -1):
            for kind in (0, 1):
                self.push(("z", d, 1, kind), at.row, kind, None, at.z_dev(d))
        self.push(("xb", 0, None), at.row, 1, None, at.x_dev())

    def partner(self):
        at = self.at
        block = at.row_at(1, 0)
        self.wire.arrived(("xa",), self.part(block, 0, None), at.x_dev())
        for d in (1, -1):
            self.push(("z", d, 1, 2), block, 0, None, at.z_dev(d))

    def step(self, s, kinds=(0, 1, 2)):
        at = self.at
        for kind in kinds:
            half = 1 if kind == 1 else 0
            for d in (1, -1):
                block = at.row_at(1 if kind == 2 else 0, -d * s)
                side = 0 if d == 1 else 1
                piece = side if s == 4 else None
                self.wire.arrived(("z", d, s, kind), self.part(block, half, piece), at.z_dev(-d))
                if s < 4:
                    self.push(("z", d, s + 1, kind), block, half, side if s == 3 else None, at.z_dev(d))
                if kind == 1:
                    self.push(("xb", -d * s, piece), block, 1, piece, at.x_dev())

    def from_x(self):
        at = self.at
        for dz in (0, -1, 1, -2, 2, -3, 3, -4, 4):
            piece = {-4: 0, 4: 1}.get(dz)
            block = at.row_at(1, dz)
            self.wire.arrived(("xb", dz, piece), self.part(block, 1, piece), at.x_dev())


def row_part(ref, size):
    half_size, piece_size = size // 2, size // 4

    def part(row, half, piece):
        start = row * size + half * half_size + (0 if piece is None else piece * piece_size)
        length = half_size if piece is None else piece_size
        return ref.at[pl.ds(pl.multiple_of(start, 16), length), :]

    return part


def col_part(ref, size):
    def part(col, piece):
        start = col * size + (0 if piece is None else piece * (size // 2))
        return ref.at[pl.ds(pl.multiple_of(start, 16), size if piece is None else size // 2), :]

    return part


def project_kernel(hidden_ref, mod_ref, onehot_ref, w_ref, q_ref, k_ref, v_ref, mod_all, w_all, stats, send_sem, recv_sem):
    at = Place()
    wire = Wire(send_sem, recv_sem)
    depth, tokens = hidden_ref.shape
    rows = RowGather(at, wire, row_part(w_all, depth))
    cols = ColGather(at, wire, col_part(mod_all, depth))
    w_all[pl.ds(pl.multiple_of(at.row * depth, 16), depth), :] = w_ref[...]
    meet(rows.peers() + [at.col_dev(i) for i in range(1, 16)])
    rows.start()

    hidden = hidden_ref[...].astype(jnp.float32)
    local_mean = jnp.sum(hidden, axis=0, keepdims=True) * (1.0 / depth)
    centred = hidden - local_mean
    local_square = jnp.sum(centred * centred, axis=0, keepdims=True)
    groups = tokens // 128
    mine = stats.at[at.col]
    mine[...] = jnp.zeros(mine.shape, jnp.float32)
    for j in range(groups):
        lanes = slice(128 * j, 128 * (j + 1))
        mine[j : j + 1, :] = local_mean[:, lanes]
        mine[8 + j : 9 + j, :] = local_square[:, lanes]
    for i in range(1, 16):
        wire.send(("stat", i), stats.at[at.col], stats.at[at.col], at.col_dev(i))
    rows.partner()
    for i in range(1, 16):
        wire.arrived(("stat", i), stats.at[(at.col - i + 16) % 16], at.col_dev(16 - i))
    means, squares = stats[:, 0:8, :], stats[:, 8:16, :]
    mean = jnp.sum(means, axis=0) * (1.0 / 16)
    apart = means - mean[None]
    total = jnp.sum(squares, axis=0) + depth * jnp.sum(apart * apart, axis=0)
    inverse = lax.rsqrt(total * (1.0 / (16 * depth)) + 1e-06)

    def as_row(packed):
        return jnp.concatenate([packed[j : j + 1, :] for j in range(groups)], axis=1)

    onehot = onehot_ref[...]
    shift = jnp.dot(mod_ref[0], onehot, preferred_element_type=jnp.float32)
    scale = jnp.dot(mod_ref[1], onehot, preferred_element_type=jnp.float32)
    modulated = (hidden_ref[...].astype(jnp.float32) - as_row(mean)) * as_row(inverse) * (1.0 + scale) + shift
    mod_all[pl.ds(pl.multiple_of(at.col * depth, 16), depth), :] = modulated.astype(jnp.bfloat16)

    cols.start()
    rows.step(1)
    cols.halves()
    cols.first(0)
    rows.step(2)
    cols.first(1)
    cols.second(0)
    rows.step(3)
    cols.second(1)
    cols.from_core()
    rows.step(4)
    rows.from_x()

    width = w_ref.shape[1]

    def tile(t, carry):
        rows_at = pl.multiple_of(t * 256, 256)
        made = contract_first(mod_all[:, pl.ds(rows_at, 256)], w_all[...]).astype(jnp.bfloat16)
        for head in range(width // (3 * HD)):
            for j, ref in enumerate((q_ref, k_ref, v_ref)):
                first = (head * 3 + j) * HD
                ref[pl.ds(rows_at, 256), head * HD : (head + 1) * HD] = made[:, first : first + HD]
        return carry

    lax.fori_loop(0, tokens // 256, tile, 0)
    wire.drain()


def project(hidden_t, mod_t, onehot_t, w_qkv):
    depth, tokens = hidden_t.shape
    width = w_qkv.shape[1]
    out = jax.ShapeDtypeStruct((tokens, width // 3), jnp.bfloat16)
    vmem = pl.BlockSpec(memory_space=pltpu.VMEM)
    return pl.pallas_call(
        project_kernel,
        out_shape=(out, out, out),
        in_specs=[vmem] * 4,
        out_specs=(vmem, vmem, vmem),
        scratch_shapes=[
            pltpu.VMEM((16 * depth, tokens), jnp.bfloat16),
            pltpu.VMEM((16 * depth, width), jnp.bfloat16),
            pltpu.VMEM((16, 16, 128), jnp.float32),
            pltpu.SemaphoreType.DMA((80,)),
            pltpu.SemaphoreType.DMA((80,)),
        ],
        compiler_params=pltpu.CompilerParams(collective_id=0, has_side_effects=True, vmem_limit_bytes=VMEM_LIMIT),
        name="project",
    )(hidden_t, mod_t, onehot_t, w_qkv)


def attend_kernel(first_ref, q_ref, low_k, own_k, high_k, low_v, own_v, high_v, prefix_ref, bounds_ref, out_ref, k_all, v_all, far, score, most):
    tokens = q_ref.shape[0]
    heads = q_ref.shape[1] // HD
    groups, slot_len = prefix_ref.shape[0], prefix_ref.shape[1]
    before = groups * slot_len
    near = 3 * tokens
    base = first_ref[0]
    starts, ends, group_of = bounds_ref[0:1, :], bounds_ref[1:2, :], bounds_ref[2:3, :]
    for g in range(groups):
        at = slice(g * slot_len, (g + 1) * slot_len)
        for h in range(heads):
            k_all[at, h * HD : (h + 1) * HD] = prefix_ref[g, :, 2 * h * HD : (2 * h + 1) * HD]
            v_all[at, h * HD : (h + 1) * HD] = prefix_ref[g, :, (2 * h + 1) * HD : (2 * h + 2) * HD]
        row = jnp.where(group_of == g, 0.0, -BIG)
        far[at, :] = jnp.broadcast_to(row, (slot_len, HD)).astype(jnp.bfloat16)
    for i, (k_ref, v_ref) in enumerate(((low_k, low_v), (own_k, own_v), (high_k, high_v))):
        at = slice(before + i * tokens, before + (i + 1) * tokens)
        k_all[at, :] = k_ref[...]
        v_all[at, :] = v_ref[...]
    place = base - tokens + lax.broadcasted_iota(jnp.int32, (near, HD), 0)
    far[before:, :] = jnp.where((starts <= place) & (place < ends), 0.0, -BIG).astype(jnp.bfloat16)

    tile = 256
    block = 256
    count = (before + near) // block
    factor = math.log2(math.e) / math.sqrt(HD)

    def one_tile(t, carry):
        rows = pl.ds(pl.multiple_of(t * tile, tile), tile)
        place = base + t * tile + lax.broadcasted_iota(jnp.int32, (tile, HD), 0)
        belongs = jnp.where((starts <= place) & (place < ends), 1.0, 0.0).astype(jnp.bfloat16)
        wide = [jnp.concatenate([q_ref[rows, h * HD : (h + 1) * HD], belongs], axis=1) for h in range(heads)]
        most[...] = jnp.full(most.shape, -BIG, jnp.float32)

        def scores(b, carry):
            keys = pl.ds(pl.multiple_of(b * block, block), block)
            for h in range(heads):
                key = jnp.concatenate([k_all[keys, h * HD : (h + 1) * HD], far[keys, :]], axis=1)
                s = lax.dot_general(wide[h], key, (((1,), (1,)), ((), ())), preferred_element_type=jnp.float32)
                score[h, b] = s
                top = most[h]
                for j in range(block // HD):
                    top = jnp.maximum(top, s[:, j * HD : (j + 1) * HD])
                most[h] = top
            return carry

        lax.fori_loop(0, count, scores, 0)
        peak = [jnp.max(most[h], axis=1, keepdims=True) * factor for h in range(heads)]

        def weigh(b, carry):
            keys = pl.ds(pl.multiple_of(b * block, block), block)
            given = []
            for h in range(heads):
                mass, summed = carry[h]
                w = jnp.exp2(score[h, b] * factor - peak[h])
                for j in range(block // HD):
                    mass = mass + w[:, j * HD : (j + 1) * HD]
                summed = summed + jnp.dot(
                    w.astype(jnp.bfloat16), v_all[keys, h * HD : (h + 1) * HD], preferred_element_type=jnp.float32
                )
                given.append((mass, summed))
            return tuple(given)

        zero = jnp.zeros((tile, HD), jnp.float32)
        done = lax.fori_loop(0, count, weigh, tuple((zero, zero) for _ in range(heads)))
        for h in range(heads):
            mass, summed = done[h]
            out_ref[rows, h * HD : (h + 1) * HD] = (summed / jnp.sum(mass, axis=1, keepdims=True)).astype(jnp.bfloat16)
        return carry

    lax.fori_loop(0, tokens // tile, one_tile, 0)


def attention(first, q, keys, values, prefix, bounds):
    tokens, width = q.shape
    total = prefix.shape[0] * prefix.shape[1] + 3 * tokens
    heads = width // HD
    vmem = pl.BlockSpec(memory_space=pltpu.VMEM)
    return pl.pallas_call(
        attend_kernel,
        out_shape=jax.ShapeDtypeStruct((tokens, width), jnp.bfloat16),
        in_specs=[pl.BlockSpec(memory_space=pltpu.SMEM)] + [vmem] * 9,
        out_specs=vmem,
        scratch_shapes=[
            pltpu.VMEM((total, width), jnp.bfloat16),
            pltpu.VMEM((total, width), jnp.bfloat16),
            pltpu.VMEM((total, HD), jnp.bfloat16),
            pltpu.VMEM((heads, total // 256, 256, 256), jnp.float32),
            pltpu.VMEM((heads, 256, HD), jnp.float32),
        ],
        compiler_params=pltpu.CompilerParams(vmem_limit_bytes=VMEM_LIMIT),
        cost_estimate=pl.CostEstimate(flops=2 * tokens * total * heads * 3 * HD, bytes_accessed=8 << 20, transcendentals=tokens * total * heads),
        name="attention",
    )(first, q, *keys, *values, prefix, bounds)


def spread_kernel(block_ref, out_ref, send_sem, recv_sem):
    at = Place()
    wire = Wire(send_sem, recv_sem)
    cols = ColGather(at, wire, col_part(out_ref, block_ref.shape[0]))
    out_ref[pl.ds(pl.multiple_of(at.col * block_ref.shape[0], 16), block_ref.shape[0]), :] = block_ref[...]
    meet(cols.peers())
    cols.start()
    cols.halves()
    cols.first(0)
    cols.first(1)
    cols.second(0)
    cols.second(1)
    cols.from_core()
    wire.drain()


def spread(block):
    vmem = pl.BlockSpec(memory_space=pltpu.VMEM)
    return pl.pallas_call(
        spread_kernel,
        out_shape=jax.ShapeDtypeStruct((16 * block.shape[0], block.shape[1]), block.dtype),
        in_specs=[vmem],
        out_specs=vmem,
        scratch_shapes=[pltpu.SemaphoreType.DMA((24,)), pltpu.SemaphoreType.DMA((24,))],
        compiler_params=pltpu.CompilerParams(collective_id=1, has_side_effects=True, vmem_limit_bytes=VMEM_LIMIT),
        name="spread",
    )(block)


def shift_rows(block):
    count = lax.axis_size("row")
    up = [(i, i + 1) for i in range(count - 1)]
    down = [(i + 1, i) for i in range(count - 1)]
    return lax.ppermute(block, "row", up), lax.ppermute(block, "row", down)


def shards(hidden_in, modulation, w_qkv, w_out, prefix_cache, req_group, req_len, owner):
    tokens, features = hidden_in.shape
    requests = req_len.shape[0]
    first = lax.axis_index("row") * tokens
    slots = lax.all_gather(prefix_cache, "row", axis=0, tiled=True)
    out_weight = lax.all_gather(w_out, "row", axis=0, tiled=True)

    earlier = jnp.arange(requests)[:, None] > jnp.arange(requests)[None, :]
    starts = jnp.sum(jnp.where(earlier, req_len[None, :], 0), axis=1)
    ends = starts + req_len
    place = first + jnp.arange(tokens, dtype=jnp.int32)
    inside = (starts[:, None] <= place[None, :]) & (place[None, :] < ends[:, None])
    onehot_t = inside.astype(jnp.bfloat16)
    mod_t = jnp.transpose(modulation[:, :2], (1, 2, 0))

    q, new_keys, new_values = project(jnp.transpose(hidden_in), mod_t, onehot_t, w_qkv)

    low_k, high_k = shift_rows(new_keys)
    low_v, high_v = shift_rows(new_values)
    pad = jnp.zeros((HD - requests,), jnp.int32)
    bounds = jnp.stack([jnp.concatenate([a, pad + fill]) for a, fill in ((starts, 1 << 30), (ends, -1), (req_group, -1))])
    bounds = jnp.concatenate([bounds, jnp.zeros((5, HD), jnp.int32)])
    prefix = jnp.concatenate([lax.dynamic_slice_in_dim(slots, owner[g], 1, 0) for g in range(owner.shape[0])])
    attended = attention(
        first.reshape(1), q, (low_k, new_keys, high_k), (low_v, new_values, high_v), prefix, bounds
    )
    gathered = spread(attended)
    parts = gathered.reshape(16, tokens, attended.shape[1])
    projected = jnp.einsum(
        "jte,jef->tf", parts, out_weight.reshape(16, attended.shape[1], features), preferred_element_type=jnp.float32
    )
    gate = jnp.dot(jnp.transpose(onehot_t), modulation[:, 2], preferred_element_type=jnp.float32)
    hidden_out = (hidden_in.astype(jnp.float32) + gate * projected).astype(jnp.bfloat16)
    return hidden_out, new_keys, new_values


def solution(mesh):
    return jax.shard_map(
        shards,
        mesh=mesh,
        in_specs=(
            P("row", "col"),
            P(None, None, "col"),
            P("row", "col"),
            P("row", "col"),
            P("row", None, "col"),
            P(),
            P(),
            P(),
        ),
        out_specs=(P("row", "col"), P("row", "col"), P("row", "col")),
        check_vma=False,
    )
```

```python
import functools
import math

import jax
import jax.numpy as jnp
from jax import lax
from jax.experimental import pallas as pl
from jax.experimental.pallas import tpu as pltpu
from jax.sharding import PartitionSpec as P

HD = 128
N_Z = 8
N_Y = 4
MESH = pl.DeviceIdType.MESH
BIG = 1e30
HALO = 672
VMEM_LIMIT = 56 << 20


def contract_first(a, b):
    return lax.dot_general(a, b, (((0,), (0,)), ((), ())), preferred_element_type=jnp.float32)


class Place:
    def __init__(self):
        self.row, self.col = lax.axis_index("row"), lax.axis_index("col")
        self.l, self.z = self.row // N_Z, self.row % N_Z
        self.h, self.y, self.k = self.col // (2 * N_Y), (self.col // 2) % N_Y, self.col % 2

    def row_at(self, plane, dz):
        l = 1 - self.l if plane else self.l
        return l * N_Z + (self.z + dz + N_Z) % N_Z

    def col_at(self, half, dy, core):
        h = 1 - self.h if half else self.h
        k = 1 - self.k if core else self.k
        return (h * N_Y + (self.y + dy + N_Y) % N_Y) * 2 + k

    def z_dev(self, dz):
        return (self.row_at(0, dz), self.col)

    def x_dev(self):
        return (self.row_at(1, 0), self.col)

    def y_dev(self, dy):
        return (self.row, self.col_at(0, dy, 0))

    def half_dev(self):
        return (self.row, self.col_at(1, 0, 0))

    def core_dev(self):
        return (self.row, self.col_at(0, 0, 1))

    def col_dev(self, offset):
        return (self.row, (self.col + offset) % 16)


class Wire:
    def __init__(self, send_sem, recv_sem):
        self.send_sem, self.recv_sem = send_sem, recv_sem
        self.index, self.sent = {}, []

    def slot(self, name):
        return self.index.setdefault(name, len(self.index))

    def copy(self, name, src, dst, dev):
        n = self.slot(name)
        return pltpu.make_async_remote_copy(
            src_ref=src,
            dst_ref=dst,
            send_sem=self.send_sem.at[n],
            recv_sem=self.recv_sem.at[n],
            device_id=dev,
            device_id_type=MESH,
        )

    def send(self, name, src, dst, dev):
        c = self.copy(name, src, dst, dev)
        c.start()
        self.sent.append(c)

    def arrived(self, name, landed, dev):
        self.copy(name, landed, landed, dev).wait_recv()

    def drain(self):
        for c in self.sent:
            c.wait_send()


def meet(devices):
    barrier = pltpu.get_barrier_semaphore()
    for dev in devices:
        pl.semaphore_signal(barrier, inc=1, device_id=dev, device_id_type=MESH)
    pl.semaphore_wait(barrier, len(devices))


class ColGather:
    def __init__(self, at, wire, part):
        self.at, self.wire, self.part = at, wire, part

    def peers(self):
        at = self.at
        return [at.y_dev(1), at.y_dev(-1), at.half_dev(), at.core_dev()]

    def push(self, name, col, piece, dev):
        self.wire.send(name, self.part(col, piece), self.part(col, piece), dev)

    def start(self):
        at = self.at
        self.push(("half",), at.col, None, at.half_dev())
        for d in (1, -1):
            self.push(("y", d, 1, 0), at.col, None, at.y_dev(d))
        self.push(("core", 0, 0, None), at.col, None, at.core_dev())

    def halves(self):
        at = self.at
        block = at.col_at(1, 0, 0)
        self.wire.arrived(("half",), self.part(block, None), at.half_dev())
        for d in (1, -1):
            self.push(("y", d, 1, 1), block, None, at.y_dev(d))
        self.push(("core", 1, 0, None), block, None, at.core_dev())

    def first(self, kind):
        at = self.at
        for d in (1, -1):
            block = at.col_at(kind, -d, 0)
            self.wire.arrived(("y", d, 1, kind), self.part(block, None), at.y_dev(-d))
            piece = 0 if d == 1 else 1
            self.push(("y", d, 2, kind), block, piece, at.y_dev(d))
            self.push(("core", kind, -d, None), block, None, at.core_dev())

    def second(self, kind):
        at = self.at
        for d in (1, -1):
            piece = 0 if d == 1 else 1
            block = at.col_at(kind, 2, 0)
            self.wire.arrived(("y", d, 2, kind), self.part(block, piece), at.y_dev(-d))
            self.push(("core", kind, 2, piece), block, piece, at.core_dev())

    def from_core(self, blocks):
        at = self.at
        for kind, dy in blocks:
            for piece in (0, 1) if dy == 2 else (None,):
                block = at.col_at(kind, dy, 1)
                self.wire.arrived(("core", kind, dy, piece), self.part(block, piece), at.core_dev())


class RowGather:
    def __init__(self, at, wire, part, tag):
        self.at, self.wire, self.part, self.tag = at, wire, part, tag

    def peers(self):
        at = self.at
        return [at.z_dev(1), at.z_dev(-1), at.x_dev()]

    def push(self, name, row, half, piece, dev):
        self.wire.send((self.tag,) + name, self.part(row, half, piece), self.part(row, half, piece), dev)

    def land(self, name, row, half, piece, dev):
        self.wire.arrived((self.tag,) + name, self.part(row, half, piece), dev)

    def start(self):
        at = self.at
        self.push(("xa",), at.row, 0, None, at.x_dev())
        for d in (1, -1):
            for kind in (0, 1):
                self.push(("z", d, 1, kind), at.row, kind, None, at.z_dev(d))
        self.push(("xb", 0, None), at.row, 1, None, at.x_dev())

    def partner(self):
        at = self.at
        block = at.row_at(1, 0)
        self.land(("xa",), block, 0, None, at.x_dev())
        for d in (1, -1):
            self.push(("z", d, 1, 2), block, 0, None, at.z_dev(d))

    def step(self, s, kinds=(0, 1, 2)):
        at = self.at
        for kind in kinds:
            half = 1 if kind == 1 else 0
            for d in (1, -1):
                block = at.row_at(1 if kind == 2 else 0, -d * s)
                side = 0 if d == 1 else 1
                piece = side if s == 4 else None
                self.land(("z", d, s, kind), block, half, piece, at.z_dev(-d))
                if s < 4:
                    self.push(("z", d, s + 1, kind), block, half, side if s == 3 else None, at.z_dev(d))
                if kind == 1:
                    self.push(("xb", -d * s, piece), block, 1, piece, at.x_dev())

    def from_x(self, offsets=(0, -1, 1, -2, 2, -3, 3, -4, 4)):
        at = self.at
        for dz in offsets:
            piece = {-4: 0, 4: 1}.get(dz)
            self.land(("xb", dz, piece), at.row_at(1, dz), 1, piece, at.x_dev())


def row_part(ref, size):
    half_size, piece_size = size // 2, size // 4

    def part(row, half, piece):
        start = row * size + half * half_size + (0 if piece is None else piece * piece_size)
        length = half_size if piece is None else piece_size
        return ref.at[pl.ds(pl.multiple_of(start, 16), length), :]

    return part


def col_part(ref, size):
    def part(col, piece):
        start = col * size + (0 if piece is None else piece * (size // 2))
        return ref.at[pl.ds(pl.multiple_of(start, 16), size if piece is None else size // 2), :]

    return part


def project_kernel(
    owner_ref, hidden_ref, mod_ref, onehot_ref, w_ref, slot_ref, q_ref, k_ref, v_ref, near_ref, prefix_ref,
    mod_all, w_all, acc, stats, pieces, send_sem, recv_sem,
):
    at = Place()
    wire = Wire(send_sem, recv_sem)
    depth, tokens = hidden_ref.shape
    width = w_ref.shape[1]
    groups = owner_ref.shape[0]
    piece = slot_ref.shape[0] // 16
    rows = RowGather(at, wire, row_part(w_all, depth), "w")
    shared = RowGather(at, wire, row_part(prefix_ref, groups * piece), "p")
    cols = ColGather(at, wire, col_part(mod_all, depth))
    row_devs = [((at.row + i) % 16, at.col) for i in range(16)]
    w_all[pl.ds(pl.multiple_of(at.row * depth, 16), depth), :] = w_ref[...]
    meet(row_devs[1:] + [at.col_dev(i) for i in range(1, 16)])
    rows.start()

    hidden = hidden_ref[...].astype(jnp.float32)
    local_mean = jnp.sum(hidden, axis=0, keepdims=True) * (1.0 / depth)
    centred = hidden - local_mean
    local_square = jnp.sum(centred * centred, axis=0, keepdims=True)
    spans = tokens // 128
    mine = stats.at[at.col]
    mine[...] = jnp.zeros(mine.shape, jnp.float32)
    for j in range(spans):
        lanes = slice(128 * j, 128 * (j + 1))
        mine[j : j + 1, :] = local_mean[:, lanes]
        mine[8 + j : 9 + j, :] = local_square[:, lanes]
    for i in range(1, 16):
        wire.send(("stat", i), stats.at[at.col], stats.at[at.col], at.col_dev(i))

    def piece_at(ref, index):
        return ref.at[pl.ds(pl.multiple_of(index * piece, 16), piece), :]

    for i in range(1, 16):
        wire.send(("slot", i), piece_at(slot_ref, (at.row + i) % 16), piece_at(pieces, at.row), row_devs[i])
    piece_at(pieces, at.row)[...] = piece_at(slot_ref, at.row)[...]
    rows.partner()
    for i in range(1, 16):
        wire.arrived(("stat", i), stats.at[(at.col - i + 16) % 16], at.col_dev(16 - i))
    means, squares = stats[:, 0:8, :], stats[:, 8:16, :]
    mean = jnp.sum(means, axis=0) * (1.0 / 16)
    apart = means - mean[None]
    total = jnp.sum(squares, axis=0) + depth * jnp.sum(apart * apart, axis=0)
    inverse = lax.rsqrt(total * (1.0 / (16 * depth)) + 1e-06)

    def as_row(packed):
        return jnp.concatenate([packed[j : j + 1, :] for j in range(spans)], axis=1)

    onehot = onehot_ref[...]
    shift = jnp.dot(mod_ref[0], onehot, preferred_element_type=jnp.float32)
    scale = jnp.dot(mod_ref[1], onehot, preferred_element_type=jnp.float32)
    modulated = (hidden_ref[...].astype(jnp.float32) - as_row(mean)) * as_row(inverse) * (1.0 + scale) + shift
    mod_all[pl.ds(pl.multiple_of(at.col * depth, 16), depth), :] = modulated.astype(jnp.bfloat16)
    cols.start()

    for i in range(1, 16):
        wire.arrived(("slot", i), piece_at(pieces, (at.row + 16 - i) % 16), row_devs[16 - i])
    from_slot = lax.broadcasted_iota(jnp.int32, (piece, 16 * piece), 1)
    own_line = lax.broadcasted_iota(jnp.int32, (piece, 16 * piece), 0)
    for g in range(groups):
        picks = jnp.where(from_slot == owner_ref[g] * piece + own_line, 1.0, 0.0).astype(jnp.bfloat16)
        chosen = jnp.dot(picks, pieces[...], preferred_element_type=jnp.float32).astype(jnp.bfloat16)
        prefix_ref[pl.ds(pl.multiple_of((at.row * groups + g) * piece, 16), piece), :] = chosen
    shared.start()

    def product(blocks, tile):
        starts = [pl.multiple_of(at.row_at(plane, dz) * depth, 16) for plane, dz in blocks]
        lanes = pl.ds(pl.multiple_of(tile * 256, 256), 256)
        left = jnp.concatenate([mod_all[pl.ds(s, depth), lanes] for s in starts], axis=0)
        right = jnp.concatenate([w_all[pl.ds(s, depth), :] for s in starts], axis=0)
        return contract_first(left, right)

    def accumulate(blocks, fresh=False):
        def one(tile, carry):
            at_rows = pl.ds(pl.multiple_of(tile * 256, 256), 256)
            made = product(blocks, tile)
            acc[at_rows, :] = made if fresh else acc[at_rows, :] + made
            return carry

        lax.fori_loop(0, tokens // 256, one, 0)

    rows.step(1)
    cols.halves()
    cols.first(0)
    shared.partner()
    rows.step(2)
    cols.first(1)
    cols.second(0)
    shared.step(1)
    rows.step(3)
    cols.second(1)
    cols.from_core([(kind, dy) for kind in (0, 1) for dy in (0, -1, 1, 2)])
    shared.step(2)
    accumulate([(0, 0), (0, -1), (0, 1), (0, -2)], True)
    rows.step(4)
    shared.step(3)
    rows.from_x((0,))
    accumulate([(0, 2), (0, -3), (0, 3), (1, 0)])
    rows.from_x((-1, 1, -2, 2))
    accumulate([(1, -1), (1, 1), (1, -2), (1, 2)])
    shared.step(4)
    rows.from_x((-3, 3, -4, 4))

    heads = width // (3 * HD)
    near = near_ref.shape[0]
    own = (near - tokens) // 2
    ahead, behind = ((at.row + 1) % 16, at.col), ((at.row + 15) % 16, at.col)
    edge = own - HALO
    near_ref[0:edge, :] = jnp.zeros((edge, near_ref.shape[1]), jnp.bfloat16)
    near_ref[near - edge : near, :] = jnp.zeros((edge, near_ref.shape[1]), jnp.bfloat16)
    spans_ahead, spans_behind = [], []
    for tile in range(tokens // 256):
        low, high = tile * 256, (tile + 1) * 256
        made = (acc[low:high, :] + product([(0, 4), (1, -3), (1, 3), (1, 4)], tile)).astype(jnp.bfloat16)
        for head in range(heads):
            first = head * 3 * HD
            lanes = slice(head * HD, (head + 1) * HD)
            q_ref[low:high, lanes] = made[:, first : first + HD]
            k_ref[low:high, lanes] = made[:, first + HD : first + 2 * HD]
            v_ref[low:high, lanes] = made[:, first + 2 * HD : first + 3 * HD]
            near_ref[own + low : own + high, 2 * head * HD : 2 * (head + 1) * HD] = made[:, first + HD : first + 3 * HD]
        begin = max(low, tokens - HALO)
        spans_ahead.append((begin, high))
        wire.send(("up", tile), near_ref.at[own + begin : own + high, :], near_ref.at[begin - tokens + own : high - tokens + own, :], ahead)
        finish = min(high, HALO)
        spans_behind.append((low, finish))
        wire.send(("down", tile), near_ref.at[own + low : own + finish, :], near_ref.at[own + tokens + low : own + tokens + finish, :], behind)
    shared.from_x()
    for tile, (begin, high) in enumerate(spans_ahead):
        wire.arrived(("up", tile), near_ref.at[begin - tokens + own : high - tokens + own, :], behind)
    for tile, (low, finish) in enumerate(spans_behind):
        wire.arrived(("down", tile), near_ref.at[own + tokens + low : own + tokens + finish, :], ahead)
    wire.drain()


def project(owner, hidden_t, mod_t, onehot_t, w_qkv, slot):
    depth, tokens = hidden_t.shape
    width = w_qkv.shape[1]
    groups, slot_len = owner.shape[0], slot.shape[0]
    heads = width // (3 * HD)

    def out(rows, columns):
        return jax.ShapeDtypeStruct((rows, columns), jnp.bfloat16)

    own = out(tokens, heads * HD)
    vmem = pl.BlockSpec(memory_space=pltpu.VMEM)
    return pl.pallas_call(
        project_kernel,
        out_shape=(own, own, own, out(3 * tokens, 2 * heads * HD), out(groups * slot_len, 2 * heads * HD)),
        in_specs=[pl.BlockSpec(memory_space=pltpu.SMEM)] + [vmem] * 5,
        out_specs=(vmem,) * 5,
        scratch_shapes=[
            pltpu.VMEM((16 * depth, tokens), jnp.bfloat16),
            pltpu.VMEM((16 * depth, width), jnp.bfloat16),
            pltpu.VMEM((tokens, width), jnp.float32),
            pltpu.VMEM((16, 16, 128), jnp.float32),
            pltpu.VMEM((slot_len, 2 * heads * HD), jnp.bfloat16),
            pltpu.SemaphoreType.DMA((128,)),
            pltpu.SemaphoreType.DMA((128,)),
        ],
        compiler_params=pltpu.CompilerParams(collective_id=0, has_side_effects=True, vmem_limit_bytes=VMEM_LIMIT),
        name="project",
    )(owner, hidden_t, mod_t, onehot_t, w_qkv, slot)


def attend_kernel(first_ref, len_ref, group_ref, q_ref, near_ref, prefix_ref, bounds_ref, out_ref, far, score, most, blocks):
    tokens = q_ref.shape[0]
    heads = q_ref.shape[1] // HD
    requests = len_ref.shape[0]
    holders, groups, piece, _ = prefix_ref.shape
    base = first_ref[0]
    starts, ends, group_of = bounds_ref[0:1, :], bounds_ref[1:2, :], bounds_ref[2:3, :]
    near = near_ref.shape[0]
    own = (near - tokens) // 2
    tile = 256; block = 256
    factor = math.log2(math.e) / math.sqrt(HD)
    place = base - own + lax.broadcasted_iota(jnp.int32, (near, HD), 0)
    far[...] = jnp.where((starts <= place) & (place < ends), 0.0, -BIG).astype(jnp.bfloat16)

    def one_tile(t, carry):
        top_pos = base + t * tile
        def scan(r, c):
            start, low, high, f = c
            end = start + len_ref[r]
            hit = (start < top_pos + tile) & (end > top_pos)
            g = group_ref[r]
            low = jnp.where(hit, jnp.minimum(low, start), low)
            high = jnp.where(hit, jnp.maximum(high, end), high)
            f = tuple(jnp.where(hit & (g == i), 1, f[i]) for i in range(groups))
            return end, low, high, f
        _, low, high, flags = lax.fori_loop(0, requests, scan, (jnp.int32(0), top_pos, top_pos, (jnp.int32(0),) * groups))
        low_block = (low - (base - own)) // block
        high_block = (high - (base - own) + block - 1) // block
        rows = pl.ds(pl.multiple_of(t * tile, tile), tile)
        place = top_pos + lax.broadcasted_iota(jnp.int32, (tile, HD), 0)
        belongs = jnp.where((starts <= place) & (place < ends), 1.0, 0.0).astype(jnp.bfloat16)
        wide = [jnp.concatenate([q_ref[rows, h * HD : (h + 1) * HD], belongs], axis=1) for h in range(heads)]
        most[...] = jnp.full(most.shape, -BIG, jnp.float32)

        def score_block(n, keys_of, mask):
            for h in range(heads):
                key = jnp.concatenate([keys_of(h), mask], axis=1)
                s = lax.dot_general(wide[h], key, (((1,), (1,)), ((), ())), preferred_element_type=jnp.float32)
                score[h, n] = s
                top = most[h]
                for j in range(block // HD):
                    top = jnp.maximum(top, s[:, j * HD : (j + 1) * HD])
                most[h] = top

        def group_part(g, j):
            return prefix_ref[:, g, :, j * HD : (j + 1) * HD].reshape(block, HD)

        used = jnp.int32(0)
        for g in range(groups):
            @pl.when(flags[g] > 0)
            def _():
                mask = jnp.broadcast_to(jnp.where(group_of == g, 0.0, -BIG), (block, HD)).astype(jnp.bfloat16)
                score_block(g, lambda h: group_part(g, 2 * h), mask)

        def near_scores(b, c):
            keys = pl.ds(pl.multiple_of(b * block, block), block)
            score_block(groups + b, lambda h: near_ref[keys, 2 * h * HD : (2 * h + 1) * HD], far[keys, :])
            return c
        lax.fori_loop(low_block, high_block, near_scores, 0)
        peak = [jnp.max(most[h], axis=1, keepdims=True) * factor for h in range(heads)]
        most[...] = jnp.zeros(most.shape, jnp.float32)
        blocks[...] = jnp.zeros(blocks.shape, jnp.float32)

        def weigh(n, values_of):
            for h in range(heads):
                w = jnp.exp2(score[h, n] * factor - peak[h])
                mass = most[h]
                for j in range(block // HD):
                    mass = mass + w[:, j * HD : (j + 1) * HD]
                most[h] = mass
                blocks[h] += jnp.dot(w.astype(jnp.bfloat16), values_of(h), preferred_element_type=jnp.float32)

        for g in range(groups):
            @pl.when(flags[g] > 0)
            def _():
                weigh(g, lambda h: group_part(g, 2 * h + 1))

        def near_weigh(b, c):
            keys = pl.ds(pl.multiple_of(b * block, block), block)
            weigh(groups + b, lambda h: near_ref[keys, (2 * h + 1) * HD : (2 * h + 2) * HD])
            return c
        lax.fori_loop(low_block, high_block, near_weigh, 0)
        for h in range(heads):
            out_ref[rows, h * HD : (h + 1) * HD] = (blocks[h] / jnp.sum(most[h], axis=1, keepdims=True)).astype(jnp.bfloat16)
        return carry
    lax.fori_loop(0, tokens // tile, one_tile, 0)

def attention(first, req_len, req_group, q, near, prefix, bounds):
    tokens, width = q.shape
    heads = width // HD
    total = near.shape[0]
    tile = 256
    vmem = pl.BlockSpec(memory_space=pltpu.VMEM)
    return pl.pallas_call(
        attend_kernel,
        out_shape=jax.ShapeDtypeStruct((tokens, width), jnp.bfloat16),
        in_specs=[pl.BlockSpec(memory_space=pltpu.SMEM)]*3 + [vmem] * 4,
        out_specs=vmem,
        scratch_shapes=[
            pltpu.VMEM((total, HD), jnp.bfloat16),
            pltpu.VMEM((heads, prefix.shape[1] + total // 256, tile, 256), jnp.float32),
            pltpu.VMEM((heads, tile, HD), jnp.float32),
            pltpu.VMEM((heads, tile, HD), jnp.float32),
        ],
        compiler_params=pltpu.CompilerParams(vmem_limit_bytes=VMEM_LIMIT),
        name="attention",
    )(first, req_len, req_group, q, near, prefix, bounds)


def output_kernel(
    block_ref, w_ref, hidden_ref, onehot_ref, gate_ref, out_ref, att_all, w_all, acc, send_sem, recv_sem
):
    at = Place()
    wire = Wire(send_sem, recv_sem)
    tokens = block_ref.shape[0]
    features = w_ref.shape[0]
    cols = ColGather(at, wire, col_part(att_all, tokens))
    rows = RowGather(at, wire, row_part(w_all, features), "w")
    meet(rows.peers() + cols.peers())
    att_all[pl.ds(pl.multiple_of(at.col * tokens, 16), tokens), :] = block_ref[...]
    cols.start()
    w_all[pl.ds(pl.multiple_of(at.row * features, 16), features), :] = w_ref[...]
    rows.start()
    gate = contract_first(onehot_ref[...], gate_ref[...])

    def accumulate(blocks, fresh=False):
        indices = [at.col_at(kind, dy, core) for kind, dy, core in blocks]
        right = jnp.concatenate([w_all[pl.ds(pl.multiple_of(i * features, 16), features), :] for i in indices], axis=1)

        def one(tile, carry):
            left = jnp.concatenate(
                [att_all[pl.ds(pl.multiple_of(i * tokens + tile * 256, 16), 256), :] for i in indices], axis=1
            )
            made = lax.dot_general(left, right, (((1,), (1,)), ((), ())), preferred_element_type=jnp.float32)
            at_rows = pl.ds(pl.multiple_of(tile * 256, 256), 256)
            acc[at_rows, :] = made if fresh else acc[at_rows, :] + made
            return carry

        lax.fori_loop(0, tokens // 256, one, 0)

    rows.partner()
    cols.halves()
    rows.step(1)
    rows.step(2)
    cols.first(0)
    rows.step(3)
    cols.first(1)
    rows.step(4)
    rows.from_x()
    cols.from_core([(0, 0), (1, 0)])
    accumulate([(0, 0, 0), (1, 0, 0), (0, 0, 1), (1, 0, 1)], True)
    cols.second(0)
    cols.second(1)
    accumulate([(0, -1, 0), (0, 1, 0), (1, -1, 0), (1, 1, 0)])
    cols.from_core([(0, -1), (0, 1), (1, -1), (1, 1)])
    accumulate([(0, -1, 1), (0, 1, 1), (1, -1, 1), (1, 1, 1)])
    cols.from_core([(0, 2), (1, 2)])
    accumulate([(0, 2, 0), (0, 2, 1), (1, 2, 0), (1, 2, 1)])
    out_ref[...] = (hidden_ref[...].astype(jnp.float32) + gate * acc[...]).astype(jnp.bfloat16)
    wire.drain()


def output(attended, w_t, hidden, onehot_t, gate):
    tokens, width = attended.shape
    features = w_t.shape[0]
    vmem = pl.BlockSpec(memory_space=pltpu.VMEM)
    return pl.pallas_call(
        output_kernel,
        out_shape=jax.ShapeDtypeStruct(hidden.shape, jnp.bfloat16),
        in_specs=[vmem] * 5,
        out_specs=vmem,
        scratch_shapes=[
            pltpu.VMEM((16 * tokens, width), jnp.bfloat16),
            pltpu.VMEM((16 * features, width), jnp.bfloat16),
            pltpu.VMEM((tokens, features), jnp.float32),
            pltpu.SemaphoreType.DMA((64,)),
            pltpu.SemaphoreType.DMA((64,)),
        ],
        compiler_params=pltpu.CompilerParams(collective_id=1, has_side_effects=True, vmem_limit_bytes=VMEM_LIMIT),
        name="output",
    )(attended, w_t, hidden, onehot_t, gate)


def shards(hidden_in, modulation, w_qkv, w_out, prefix_cache, req_group, req_len, owner):
    tokens, features = hidden_in.shape
    requests = req_len.shape[0]
    groups, slot_len = owner.shape[0], prefix_cache.shape[1]
    first = lax.axis_index("row") * tokens
    earlier = jnp.arange(requests)[:, None] > jnp.arange(requests)[None, :]
    starts = jnp.sum(jnp.where(earlier, req_len[None, :], 0), axis=1)
    ends = starts + req_len
    place = first + jnp.arange(tokens, dtype=jnp.int32)
    inside = (starts[:, None] <= place[None, :]) & (place[None, :] < ends[:, None])
    onehot_t = inside.astype(jnp.bfloat16)
    mod_t = jnp.transpose(modulation[:, :2], (1, 2, 0))
    q, new_keys, new_values, near, prefix = project(
        owner, jnp.transpose(hidden_in), mod_t, onehot_t, w_qkv, prefix_cache[0]
    )
    pad = jnp.zeros((HD - requests,), jnp.int32)
    bounds = jnp.stack([jnp.concatenate([a, pad + fill]) for a, fill in ((starts, 1 << 30), (ends, -1), (req_group, -1))])
    bounds = jnp.concatenate([bounds, jnp.zeros((5, HD), jnp.int32)])
    prefix = prefix.reshape(16, groups, slot_len // 16, prefix.shape[1])
    attended = attention(first.reshape(1), req_len, req_group, q, near, prefix, bounds)
    hidden_out = output(attended, jnp.transpose(w_out), hidden_in, onehot_t, modulation[:, 2])
    return hidden_out, new_keys, new_values


def solution(mesh):
    return jax.shard_map(
        shards,
        mesh=mesh,
        in_specs=(
            P("row", "col"),
            P(None, None, "col"),
            P("row", "col"),
            P("row", "col"),
            P("row", None, "col"),
            P(),
            P(),
            P(),
        ),
        out_specs=(P("row", "col"), P("row", "col"), P("row", "col")),
        check_vma=False,
    )
```

```python
import math

import jax
import jax.numpy as jnp
from jax import lax
from jax.experimental import pallas as pl
from jax.experimental.pallas import tpu as pltpu
from jax.sharding import PartitionSpec as P

HD = 128
N_Z = 8
N_Y = 4
MESH = pl.DeviceIdType.MESH
BIG = 1e30
HALO = 672
VMEM_LIMIT = 60 << 20
TILE = 256


def contract_first(a, b):
    return lax.dot_general(a, b, (((0,), (0,)), ((), ())), preferred_element_type=jnp.float32)


class Place:
    def __init__(self):
        self.row, self.col = lax.axis_index("row"), lax.axis_index("col")
        self.l, self.z = self.row // N_Z, self.row % N_Z
        self.h, self.y, self.k = self.col // (2 * N_Y), (self.col // 2) % N_Y, self.col % 2

    def row_at(self, plane, dz):
        l = 1 - self.l if plane else self.l
        return l * N_Z + (self.z + dz + N_Z) % N_Z

    def col_at(self, half, dy, core):
        h = 1 - self.h if half else self.h
        k = 1 - self.k if core else self.k
        return (h * N_Y + (self.y + dy + N_Y) % N_Y) * 2 + k

    def z_dev(self, dz):
        return (self.row_at(0, dz), self.col)

    def x_dev(self):
        return (self.row_at(1, 0), self.col)

    def y_dev(self, dy):
        return (self.row, self.col_at(0, dy, 0))

    def half_dev(self):
        return (self.row, self.col_at(1, 0, 0))

    def core_dev(self):
        return (self.row, self.col_at(0, 0, 1))

    def col_dev(self, offset):
        return (self.row, (self.col + offset) % 16)


class Wire:
    def __init__(self, send_sem, recv_sem):
        self.send_sem, self.recv_sem = send_sem, recv_sem
        self.index, self.sent = {}, []

    def slot(self, name):
        return self.index.setdefault(name, len(self.index))

    def copy(self, name, src, dst, dev):
        n = self.slot(name)
        return pltpu.make_async_remote_copy(
            src_ref=src,
            dst_ref=dst,
            send_sem=self.send_sem.at[n],
            recv_sem=self.recv_sem.at[n],
            device_id=dev,
            device_id_type=MESH,
        )

    def send(self, name, src, dst, dev):
        c = self.copy(name, src, dst, dev)
        c.start()
        self.sent.append(c)

    def arrived(self, name, landed, dev):
        self.copy(name, landed, landed, dev).wait_recv()

    def drain(self):
        for c in self.sent:
            c.wait_send()


def meet(devices):
    barrier = pltpu.get_barrier_semaphore()
    for dev in devices:
        pl.semaphore_signal(barrier, inc=1, device_id=dev, device_id_type=MESH)
    pl.semaphore_wait(barrier, len(devices))


class ColGather:
    def __init__(self, at, wire, part, tag):
        self.at, self.wire, self.part, self.tag = at, wire, part, tag

    def peers(self):
        at = self.at
        return [at.y_dev(1), at.y_dev(-1), at.half_dev(), at.core_dev()]

    def push(self, name, col, piece, dev):
        self.wire.send((self.tag,) + name, self.part(col, piece), self.part(col, piece), dev)

    def land(self, name, col, piece, dev):
        self.wire.arrived((self.tag,) + name, self.part(col, piece), dev)

    def start(self):
        at = self.at
        self.push(("half",), at.col, None, at.half_dev())
        for d in (1, -1):
            self.push(("y", d, 1, 0), at.col, None, at.y_dev(d))
        self.push(("core", 0, 0, None), at.col, None, at.core_dev())

    def halves(self):
        at = self.at
        block = at.col_at(1, 0, 0)
        self.land(("half",), block, None, at.half_dev())
        for d in (1, -1):
            self.push(("y", d, 1, 1), block, None, at.y_dev(d))
        self.push(("core", 1, 0, None), block, None, at.core_dev())

    def first(self, kind):
        at = self.at
        for d in (1, -1):
            block = at.col_at(kind, -d, 0)
            self.land(("y", d, 1, kind), block, None, at.y_dev(-d))
            self.push(("y", d, 2, kind), block, 0 if d == 1 else 1, at.y_dev(d))
            self.push(("core", kind, -d, None), block, None, at.core_dev())

    def second(self, kind):
        at = self.at
        for d in (1, -1):
            piece = 0 if d == 1 else 1
            block = at.col_at(kind, 2, 0)
            self.land(("y", d, 2, kind), block, piece, at.y_dev(-d))
            self.push(("core", kind, 2, piece), block, piece, at.core_dev())

    def from_core(self):
        at = self.at
        for kind, dy in ((0, 0), (1, 0), (0, -1), (0, 1), (1, -1), (1, 1), (0, 2), (1, 2)):
            for piece in (0, 1) if dy == 2 else (None,):
                self.land(("core", kind, dy, piece), at.col_at(kind, dy, 1), piece, at.core_dev())


class RowGather:
    def __init__(self, at, wire, part, tag):
        self.at, self.wire, self.part, self.tag = at, wire, part, tag

    def peers(self):
        at = self.at
        return [at.z_dev(1), at.z_dev(-1), at.x_dev()]

    def push(self, name, row, half, piece, dev):
        self.wire.send((self.tag,) + name, self.part(row, half, piece), self.part(row, half, piece), dev)

    def land(self, name, row, half, piece, dev):
        self.wire.arrived((self.tag,) + name, self.part(row, half, piece), dev)

    def start(self):
        at = self.at
        self.push(("xa",), at.row, 0, None, at.x_dev())
        for d in (1, -1):
            for kind in (0, 1):
                self.push(("z", d, 1, kind), at.row, kind, None, at.z_dev(d))
        self.push(("xb", 0, None), at.row, 1, None, at.x_dev())

    def partner(self):
        at = self.at
        block = at.row_at(1, 0)
        self.land(("xa",), block, 0, None, at.x_dev())
        for d in (1, -1):
            self.push(("z", d, 1, 2), block, 0, None, at.z_dev(d))

    def step(self, s, kinds=(0, 1, 2)):
        at = self.at
        for kind in kinds:
            half = 1 if kind == 1 else 0
            for d in (1, -1):
                block = at.row_at(1 if kind == 2 else 0, -d * s)
                side = 0 if d == 1 else 1
                piece = side if s == 4 else None
                self.land(("z", d, s, kind), block, half, piece, at.z_dev(-d))
                if s < 4:
                    self.push(("z", d, s + 1, kind), block, half, side if s == 3 else None, at.z_dev(d))
                if kind == 1:
                    self.push(("xb", -d * s, piece), block, 1, piece, at.x_dev())

    def from_x(self, offsets=(0, -1, 1, -2, 2, -3, 3, -4, 4)):
        at = self.at
        for dz in offsets:
            piece = {-4: 0, 4: 1}.get(dz)
            self.land(("xb", dz, piece), at.row_at(1, dz), 1, piece, at.x_dev())


def row_part(ref, size, crossing):
    def part(row, half, piece):
        length = size - crossing if half else crossing
        start = row * size + half * crossing
        if piece is not None:
            length = length // 2
            start = start + piece * length
        return ref.at[pl.ds(pl.multiple_of(start, 16), length), :]

    return part


def col_part(ref, size, offset=0, length=None):
    length = size if length is None else length

    def part(col, piece):
        start = col * size + offset + (0 if piece is None else piece * (length // 2))
        return ref.at[pl.ds(pl.multiple_of(start, 16), length if piece is None else length // 2), :]

    return part


def request_bounds(len_ref, group_ref, base, tokens):
    requests = len_ref.shape[0]
    line = lax.broadcasted_iota(jnp.int32, (requests, HD), 0)
    lane = lax.broadcasted_iota(jnp.int32, (8, HD), 1)

    def bound(r, carry):
        start, start_col, end_col, start_row, end_row, group_row = carry
        end = start + len_ref[r]
        here, there = line == r, lane == r
        return (
            end,
            jnp.where(here, start, start_col),
            jnp.where(here, end, end_col),
            jnp.where(there, start, start_row),
            jnp.where(there, end, end_row),
            jnp.where(there, group_ref[r], group_row),
        )

    column = jnp.zeros((requests, HD), jnp.int32)
    flat = jnp.full((8, HD), -1, jnp.int32)
    _, start_col, end_col, start_row, end_row, group_row = lax.fori_loop(
        0, requests, bound, (jnp.int32(0), column, column, flat, flat, flat)
    )
    start_row, end_row, group_row = start_row[0:1], end_row[0:1], group_row[0:1]
    place = base + lax.broadcasted_iota(jnp.int32, (requests, tokens), 1)
    begins = jnp.concatenate([start_col] * (tokens // HD), axis=1)
    ends = jnp.concatenate([end_col] * (tokens // HD), axis=1)
    onehot = jnp.where((begins <= place) & (place < ends), 1.0, 0.0).astype(jnp.bfloat16)
    return start_row, end_row, group_row, onehot


def project_kernel(
    owner_ref, hidden_ref, mod_ref, onehot_ref, w_ref, slot_ref, q_ref, k_ref, v_ref, near_ref, prefix_ref,
    mod_all, w_all, acc, stats, pieces, send_sem, recv_sem,
):
    at = Place()
    wire = Wire(send_sem, recv_sem)
    depth, tokens = hidden_ref.shape
    width = w_ref.shape[1]
    groups = owner_ref.shape[0]
    piece = slot_ref.shape[0] // 16
    rows = RowGather(at, wire, row_part(w_all, depth, 128), "w")
    shared = RowGather(at, wire, row_part(prefix_ref, groups * piece, groups * piece // 2), "p")
    cols = ColGather(at, wire, col_part(mod_all, depth), "m")
    row_devs = [((at.row + i) % 16, at.col) for i in range(16)]
    w_all[pl.ds(pl.multiple_of(at.row * depth, 16), depth), :] = w_ref[...]
    meet(row_devs[1:] + [at.col_dev(i) for i in range(1, 16)])
    rows.start()

    hidden = hidden_ref[...].astype(jnp.float32)
    local_mean = jnp.sum(hidden, axis=0, keepdims=True) * (1.0 / depth)
    centred = hidden - local_mean
    local_square = jnp.sum(centred * centred, axis=0, keepdims=True)
    spans = tokens // 128
    mine = stats.at[at.col]
    mine[...] = jnp.zeros(mine.shape, jnp.float32)
    for j in range(spans):
        lanes = slice(128 * j, 128 * (j + 1))
        mine[j : j + 1, :] = local_mean[:, lanes]
        mine[8 + j : 9 + j, :] = local_square[:, lanes]
    for i in range(1, 16):
        wire.send(("stat", i), stats.at[at.col], stats.at[at.col], at.col_dev(i))

    def piece_at(ref, index):
        return ref.at[pl.ds(pl.multiple_of(index * piece, 16), piece), :]

    for i in range(1, 16):
        wire.send(("slot", i), piece_at(slot_ref, (at.row + i) % 16), piece_at(pieces, at.row), row_devs[i])
    piece_at(pieces, at.row)[...] = piece_at(slot_ref, at.row)[...]
    rows.partner()
    for i in range(1, 16):
        wire.arrived(("stat", i), stats.at[(at.col - i + 16) % 16], at.col_dev(16 - i))
    means, squares = stats[:, 0:8, :], stats[:, 8:16, :]
    mean = jnp.sum(means, axis=0) * (1.0 / 16)
    apart = means - mean[None]
    total = jnp.sum(squares, axis=0) + depth * jnp.sum(apart * apart, axis=0)
    inverse = lax.rsqrt(total * (1.0 / (16 * depth)) + 1e-06)

    def as_row(packed):
        return jnp.concatenate([packed[j : j + 1, :] for j in range(spans)], axis=1)

    onehot = onehot_ref[...]
    shift = jnp.dot(mod_ref[0], onehot, preferred_element_type=jnp.float32)
    scale = jnp.dot(mod_ref[1], onehot, preferred_element_type=jnp.float32)
    modulated = (hidden_ref[...].astype(jnp.float32) - as_row(mean)) * as_row(inverse) * (1.0 + scale) + shift
    mod_all[pl.ds(pl.multiple_of(at.col * depth, 16), depth), :] = modulated.astype(jnp.bfloat16)
    cols.start()

    for i in range(1, 16):
        wire.arrived(("slot", i), piece_at(pieces, (at.row + 16 - i) % 16), row_devs[16 - i])
    from_slot = lax.broadcasted_iota(jnp.int32, (piece, 16 * piece), 1)
    own_line = lax.broadcasted_iota(jnp.int32, (piece, 16 * piece), 0)
    for g in range(groups):
        picks = jnp.where(from_slot == owner_ref[g] * piece + own_line, 1.0, 0.0).astype(jnp.bfloat16)
        chosen = jnp.dot(picks, pieces[...], preferred_element_type=jnp.float32).astype(jnp.bfloat16)
        prefix_ref[pl.ds(pl.multiple_of((at.row * groups + g) * piece, 16), piece), :] = chosen
    shared.start()

    def product(blocks, tile):
        starts = [pl.multiple_of(at.row_at(plane, dz) * depth, 16) for plane, dz in blocks]
        lanes = pl.ds(pl.multiple_of(tile * 256, 256), 256)
        left = jnp.concatenate([mod_all[pl.ds(s, depth), lanes] for s in starts], axis=0)
        right = jnp.concatenate([w_all[pl.ds(s, depth), :] for s in starts], axis=0)
        return contract_first(left, right)

    def accumulate(blocks, fresh=False):
        def one(tile, carry):
            at_rows = pl.ds(pl.multiple_of(tile * 256, 256), 256)
            made = product(blocks, tile)
            acc[at_rows, :] = made if fresh else acc[at_rows, :] + made
            return carry

        lax.fori_loop(0, tokens // 256, one, 0)

    rows.step(1)
    cols.halves()
    cols.first(0)
    shared.partner()
    rows.step(2)
    cols.first(1)
    cols.second(0)
    shared.step(1)
    rows.step(3)
    cols.second(1)
    cols.from_core()
    shared.step(2)
    accumulate([(0, 0), (0, -1), (0, 1), (0, -2)], True)
    rows.step(4)
    shared.step(3)
    rows.from_x((0,))
    accumulate([(0, 2), (0, -3), (0, 3), (1, 0)])
    rows.from_x((-1, 1, -2, 2))
    accumulate([(1, -1), (1, 1), (1, -2), (1, 2)])
    shared.step(4)
    rows.from_x((-3, 3, -4, 4))

    heads = width // (3 * HD)
    near = near_ref.shape[0]
    own = (near - tokens) // 2
    ahead, behind = ((at.row + 1) % 16, at.col), ((at.row + 15) % 16, at.col)
    edge = own - HALO
    near_ref[0:edge, :] = jnp.zeros((edge, near_ref.shape[1]), jnp.bfloat16)
    near_ref[near - edge : near, :] = jnp.zeros((edge, near_ref.shape[1]), jnp.bfloat16)
    spans_ahead, spans_behind = [], []
    for tile in range(tokens // 256):
        low, high = tile * 256, (tile + 1) * 256
        made = (acc[low:high, :] + product([(0, 4), (1, -3), (1, 3), (1, 4)], tile)).astype(jnp.bfloat16)
        for head in range(heads):
            first = head * 3 * HD
            lanes = slice(head * HD, (head + 1) * HD)
            q_ref[low:high, lanes] = made[:, first : first + HD]
            k_ref[low:high, lanes] = made[:, first + HD : first + 2 * HD]
            v_ref[low:high, lanes] = made[:, first + 2 * HD : first + 3 * HD]
            near_ref[own + low : own + high, 2 * head * HD : 2 * (head + 1) * HD] = made[:, first + HD : first + 3 * HD]
        begin = max(low, tokens - HALO)
        spans_ahead.append((begin, high))
        wire.send(("up", tile), near_ref.at[own + begin : own + high, :], near_ref.at[begin - tokens + own : high - tokens + own, :], ahead)
        finish = min(high, HALO)
        spans_behind.append((low, finish))
        wire.send(("down", tile), near_ref.at[own + low : own + finish, :], near_ref.at[own + tokens + low : own + tokens + finish, :], behind)
    shared.from_x()
    for tile, (begin, high) in enumerate(spans_ahead):
        wire.arrived(("up", tile), near_ref.at[begin - tokens + own : high - tokens + own, :], behind)
    for tile, (low, finish) in enumerate(spans_behind):
        wire.arrived(("down", tile), near_ref.at[own + tokens + low : own + tokens + finish, :], ahead)
    wire.drain()


def project(owner, hidden_t, mod_t, onehot_t, w_qkv, slot):
    depth, tokens = hidden_t.shape
    width = w_qkv.shape[1]
    groups, slot_len = owner.shape[0], slot.shape[0]
    heads = width // (3 * HD)

    def out(rows, columns):
        return jax.ShapeDtypeStruct((rows, columns), jnp.bfloat16)

    own = out(tokens, heads * HD)
    vmem = pl.BlockSpec(memory_space=pltpu.VMEM)
    return pl.pallas_call(
        project_kernel,
        out_shape=(own, own, own, out(3 * tokens, 2 * heads * HD), out(groups * slot_len, 2 * heads * HD)),
        in_specs=[pl.BlockSpec(memory_space=pltpu.SMEM)] + [vmem] * 5,
        out_specs=(vmem,) * 5,
        scratch_shapes=[
            pltpu.VMEM((16 * depth, tokens), jnp.bfloat16),
            pltpu.VMEM((16 * depth, width), jnp.bfloat16),
            pltpu.VMEM((tokens, width), jnp.float32),
            pltpu.VMEM((16, 16, 128), jnp.float32),
            pltpu.VMEM((slot_len, 2 * heads * HD), jnp.bfloat16),
            pltpu.SemaphoreType.DMA((128,)),
            pltpu.SemaphoreType.DMA((128,)),
        ],
        compiler_params=pltpu.CompilerParams(collective_id=0, has_side_effects=True, vmem_limit_bytes=VMEM_LIMIT),
        name="project",
    )(owner, hidden_t, mod_t, onehot_t, w_qkv, slot)


def attend_kernel(
    len_ref, group_ref, mod_ref, w_out_ref, hidden_ref, q_all, near, prefix, out_ref,
    far, far_prefix, att_all, w_out_all, send_sem, recv_sem,
):
    at = Place()
    wire = Wire(send_sem, recv_sem)
    tokens = q_all.shape[0]
    heads = q_all.shape[1] // HD
    features = w_out_ref.shape[0]
    tiles = tokens // TILE
    groups = 4
    piece = prefix.shape[0] // (16 * groups)
    weights = RowGather(at, wire, row_part(w_out_all, features, features // 2), "o")
    outs = [ColGather(at, wire, col_part(att_all, tokens, t * TILE, TILE), ("a", t)) for t in range(tiles)]

    def span(start, length):
        return pl.ds(pl.multiple_of(start, 16), length)

    w_out_all[span(at.row * features, features), :] = w_out_ref[...]
    meet(weights.peers() + outs[0].peers())
    weights.start()
    base = at.row * tokens
    start_row, end_row, group_row, onehot = request_bounds(len_ref, group_ref, base, tokens)
    near_len = near.shape[0]
    own = (near_len - tokens) // 2
    spot = base - own + lax.broadcasted_iota(jnp.int32, (near_len, HD), 0)
    far[...] = jnp.where((start_row <= spot) & (spot < end_row), 0.0, -BIG).astype(jnp.bfloat16)
    held = [jnp.broadcast_to(jnp.where(group_row == g, 0.0, -BIG), (piece, HD)) for g in range(groups)]
    held = jnp.concatenate(held, axis=0).astype(jnp.bfloat16)
    for r in range(16):
        far_prefix[r * groups * piece : (r + 1) * groups * piece, :] = held
    weights.partner()
    factor = math.log2(math.e) / math.sqrt(HD)
    window = TILE + 2 * (HALO + 32)

    def attend(t):
        place = base + t * TILE + lax.broadcasted_iota(jnp.int32, (TILE, HD), 0)
        belongs = jnp.where((start_row <= place) & (place < end_row), 1.0, 0.0).astype(jnp.bfloat16)
        seen = slice(own + t * TILE - HALO - 32, own + t * TILE - HALO - 32 + window)
        made = []
        hidden_from = jnp.concatenate([far_prefix[...], far[seen, :]], axis=0)
        for h in range(heads):
            lanes = slice(h * HD, (h + 1) * HD)
            of_key, of_value = slice(2 * h * HD, (2 * h + 1) * HD), slice((2 * h + 1) * HD, (2 * h + 2) * HD)
            query = jnp.concatenate([q_all[t * TILE : (t + 1) * TILE, lanes], belongs], axis=1)
            key = jnp.concatenate([jnp.concatenate([prefix[:, of_key], near[seen, of_key]], axis=0), hidden_from], axis=1)
            score = lax.dot_general(query, key, (((1,), (1,)), ((), ())), preferred_element_type=jnp.float32)
            peak = jnp.max(score, axis=1, keepdims=True) * factor
            weight = jnp.exp2(score * factor - peak)
            mass = jnp.sum(weight, axis=1, keepdims=True)
            value = jnp.concatenate([prefix[:, of_value], near[seen, of_value]], axis=0)
            summed = jnp.dot(weight.astype(jnp.bfloat16), value, preferred_element_type=jnp.float32)
            made.append((summed / mass).astype(jnp.bfloat16))
        att_all[span(at.col * tokens + t * TILE, TILE), :] = jnp.concatenate(made, axis=1)
        outs[t].start()

    attend(0)
    weights.step(1)
    attend(1)
    outs[0].halves()
    outs[0].first(0)
    weights.step(2)
    attend(2)
    outs[0].first(1)
    outs[1].halves()
    outs[1].first(0)
    weights.step(3)
    outs[0].second(0)
    outs[1].first(1)
    outs[2].halves()
    outs[0].second(1)
    outs[2].first(0)
    weights.step(4)
    outs[1].second(0)
    outs[2].first(1)
    outs[1].second(1)
    weights.from_x()
    gate = contract_first(onehot, mod_ref[2])
    right = jnp.concatenate([w_out_all[j * features : (j + 1) * features, :] for j in range(16)], axis=1)

    def finish_tile(t):
        low, high = t * TILE, (t + 1) * TILE
        outs[t].from_core()
        left = jnp.concatenate([att_all[j * tokens + low : j * tokens + high, :] for j in range(16)], axis=1)
        made = lax.dot_general(left, right, (((1,), (1,)), ((), ())), preferred_element_type=jnp.float32)
        out_ref[low:high, :] = (hidden_ref[low:high, :].astype(jnp.float32) + gate[low:high, :] * made).astype(jnp.bfloat16)

    finish_tile(0)
    outs[2].second(0)
    outs[2].second(1)
    finish_tile(1)
    finish_tile(2)
    wire.drain()


def attend(req_len, req_group, mod, w_out_t, hidden, q, near, prefix):
    tokens, own = q.shape
    features = hidden.shape[1]
    vmem = pl.BlockSpec(memory_space=pltpu.VMEM)
    return pl.pallas_call(
        attend_kernel,
        out_shape=jax.ShapeDtypeStruct(hidden.shape, jnp.bfloat16),
        in_specs=[pl.BlockSpec(memory_space=pltpu.SMEM)] * 2 + [vmem] * 6,
        out_specs=vmem,
        scratch_shapes=[
            pltpu.VMEM((near.shape[0], HD), jnp.bfloat16),
            pltpu.VMEM((prefix.shape[0], HD), jnp.bfloat16),
            pltpu.VMEM((16 * tokens, own), jnp.bfloat16),
            pltpu.VMEM((16 * features, own), jnp.bfloat16),
            pltpu.SemaphoreType.DMA((96,)),
            pltpu.SemaphoreType.DMA((96,)),
        ],
        compiler_params=pltpu.CompilerParams(collective_id=1, has_side_effects=True, vmem_limit_bytes=VMEM_LIMIT),
        name="attend",
    )(req_len, req_group, mod, w_out_t, hidden, q, near, prefix)


def shards(hidden_in, modulation, w_qkv, w_out, prefix_cache, req_group, req_len, owner):
    tokens = hidden_in.shape[0]
    requests = req_len.shape[0]
    first = lax.axis_index("row") * tokens
    earlier = jnp.arange(requests)[:, None] > jnp.arange(requests)[None, :]
    starts = jnp.sum(jnp.where(earlier, req_len[None, :], 0), axis=1)
    ends = starts + req_len
    place = first + jnp.arange(tokens, dtype=jnp.int32)
    inside = (starts[:, None] <= place[None, :]) & (place[None, :] < ends[:, None])
    onehot_t = inside.astype(jnp.bfloat16)
    mod_t = jnp.transpose(modulation[:, :2], (1, 2, 0))
    q, new_keys, new_values, near, prefix = project(
        owner, jnp.transpose(hidden_in), mod_t, onehot_t, w_qkv, prefix_cache[0]
    )
    mod = jnp.transpose(modulation, (1, 0, 2))
    hidden_out = attend(req_len, req_group, mod, jnp.transpose(w_out), hidden_in, q, near, prefix)
    return hidden_out, new_keys, new_values


def solution(mesh):
    return jax.shard_map(
        shards,
        mesh=mesh,
        in_specs=(
            P("row", "col"),
            P(None, None, "col"),
            P("row", "col"),
            P("row", "col"),
            P("row", None, "col"),
            P(),
            P(),
            P(),
        ),
        out_specs=(P("row", "col"), P("row", "col"), P("row", "col")),
        check_vma=False,
    )
```

```python
import math

import jax
import jax.numpy as jnp
from jax import lax
from jax.experimental import pallas as pl
from jax.experimental.pallas import tpu as pltpu
from jax.sharding import PartitionSpec as P

HD = 128
N_Z = 8
N_Y = 4
MESH = pl.DeviceIdType.MESH
BIG = 1e30
HALO = 672
VMEM_LIMIT = 60 << 20
TILE = 256


def contract_first(a, b):
    return lax.dot_general(a, b, (((0,), (0,)), ((), ())), preferred_element_type=jnp.float32)


class Place:
    def __init__(self):
        self.row, self.col = lax.axis_index("row"), lax.axis_index("col")
        self.l, self.z = self.row // N_Z, self.row % N_Z
        self.h, self.y, self.k = self.col // (2 * N_Y), (self.col // 2) % N_Y, self.col % 2

    def row_at(self, plane, dz):
        l = 1 - self.l if plane else self.l
        return l * N_Z + (self.z + dz + N_Z) % N_Z

    def col_at(self, half, dy, core):
        h = 1 - self.h if half else self.h
        k = 1 - self.k if core else self.k
        return (h * N_Y + (self.y + dy + N_Y) % N_Y) * 2 + k

    def z_dev(self, dz):
        return (self.row_at(0, dz), self.col)

    def x_dev(self):
        return (self.row_at(1, 0), self.col)

    def y_dev(self, dy):
        return (self.row, self.col_at(0, dy, 0))

    def half_dev(self):
        return (self.row, self.col_at(1, 0, 0))

    def core_dev(self):
        return (self.row, self.col_at(0, 0, 1))

    def col_dev(self, offset):
        return (self.row, (self.col + offset) % 16)


class Wire:
    def __init__(self, send_sem, recv_sem):
        self.send_sem, self.recv_sem = send_sem, recv_sem
        self.index, self.sent = {}, []

    def slot(self, name):
        return self.index.setdefault(name, len(self.index))

    def copy(self, name, src, dst, dev):
        n = self.slot(name)
        return pltpu.make_async_remote_copy(
            src_ref=src,
            dst_ref=dst,
            send_sem=self.send_sem.at[n],
            recv_sem=self.recv_sem.at[n],
            device_id=dev,
            device_id_type=MESH,
        )

    def send(self, name, src, dst, dev):
        c = self.copy(name, src, dst, dev)
        c.start()
        self.sent.append(c)

    def arrived(self, name, landed, dev):
        self.copy(name, landed, landed, dev).wait_recv()

    def drain(self):
        for c in self.sent:
            c.wait_send()


def greet(devices):
    barrier = pltpu.get_barrier_semaphore()
    for dev in devices:
        pl.semaphore_signal(barrier, inc=1, device_id=dev, device_id_type=MESH)


def meet(devices):
    pl.semaphore_wait(pltpu.get_barrier_semaphore(), len(devices))


class ColGather:
    def __init__(self, at, wire, part, tag):
        self.at, self.wire, self.part, self.tag = at, wire, part, tag

    def peers(self):
        at = self.at
        return [at.y_dev(1), at.y_dev(-1), at.half_dev(), at.core_dev()]

    def push(self, name, col, piece, dev):
        self.wire.send((self.tag,) + name, self.part(col, piece), self.part(col, piece), dev)

    def land(self, name, col, piece, dev):
        self.wire.arrived((self.tag,) + name, self.part(col, piece), dev)

    def start(self):
        at = self.at
        self.push(("half",), at.col, None, at.half_dev())
        for d in (1, -1):
            self.push(("y", d, 1, 0), at.col, None, at.y_dev(d))
        self.push(("core", 0, 0, None), at.col, None, at.core_dev())

    def halves(self):
        at = self.at
        block = at.col_at(1, 0, 0)
        self.land(("half",), block, None, at.half_dev())
        for d in (1, -1):
            self.push(("y", d, 1, 1), block, None, at.y_dev(d))
        self.push(("core", 1, 0, None), block, None, at.core_dev())

    def first(self, kind):
        at = self.at
        for d in (1, -1):
            block = at.col_at(kind, -d, 0)
            self.land(("y", d, 1, kind), block, None, at.y_dev(-d))
            self.push(("y", d, 2, kind), block, 0 if d == 1 else 1, at.y_dev(d))
            self.push(("core", kind, -d, None), block, None, at.core_dev())

    def second(self, kind):
        at = self.at
        for d in (1, -1):
            piece = 0 if d == 1 else 1
            block = at.col_at(kind, 2, 0)
            self.land(("y", d, 2, kind), block, piece, at.y_dev(-d))
            self.push(("core", kind, 2, piece), block, piece, at.core_dev())

    def from_core(self):
        at = self.at
        for kind, dy in ((0, 0), (1, 0), (0, -1), (0, 1), (1, -1), (1, 1), (0, 2), (1, 2)):
            for piece in (0, 1) if dy == 2 else (None,):
                self.land(("core", kind, dy, piece), at.col_at(kind, dy, 1), piece, at.core_dev())


class RowGather:
    def __init__(self, at, wire, part, tag):
        self.at, self.wire, self.part, self.tag = at, wire, part, tag

    def peers(self):
        at = self.at
        return [at.z_dev(1), at.z_dev(-1), at.x_dev()]

    def push(self, name, row, half, piece, dev):
        self.wire.send((self.tag,) + name, self.part(row, half, piece), self.part(row, half, piece), dev)

    def land(self, name, row, half, piece, dev):
        self.wire.arrived((self.tag,) + name, self.part(row, half, piece), dev)

    def start(self):
        at = self.at
        self.push(("xa",), at.row, 0, None, at.x_dev())
        for d in (1, -1):
            for kind in (0, 1):
                self.push(("z", d, 1, kind), at.row, kind, None, at.z_dev(d))
        self.push(("xb", 0, None), at.row, 1, None, at.x_dev())

    def partner(self):
        at = self.at
        block = at.row_at(1, 0)
        self.land(("xa",), block, 0, None, at.x_dev())
        for d in (1, -1):
            self.push(("z", d, 1, 2), block, 0, None, at.z_dev(d))

    def step(self, s, kinds=(0, 1, 2)):
        at = self.at
        for kind in kinds:
            half = 1 if kind == 1 else 0
            for d in (1, -1):
                block = at.row_at(1 if kind == 2 else 0, -d * s)
                side = 0 if d == 1 else 1
                piece = side if s == 4 else None
                self.land(("z", d, s, kind), block, half, piece, at.z_dev(-d))
                if s < 4:
                    self.push(("z", d, s + 1, kind), block, half, side if s == 3 else None, at.z_dev(d))
                if kind == 1:
                    self.push(("xb", -d * s, piece), block, 1, piece, at.x_dev())

    def from_x(self, offsets=(0, -1, 1, -2, 2, -3, 3, -4, 4)):
        at = self.at
        for dz in offsets:
            piece = {-4: 0, 4: 1}.get(dz)
            self.land(("xb", dz, piece), at.row_at(1, dz), 1, piece, at.x_dev())


def row_part(ref, size, crossing):
    def part(row, half, piece):
        length = size - crossing if half else crossing
        start = row * size + half * crossing
        if piece is not None:
            length = length // 2
            start = start + piece * length
        return ref.at[pl.ds(pl.multiple_of(start, 16), length), :]

    return part


def col_part(ref, size, offset=0, length=None):
    length = size if length is None else length

    def part(col, piece):
        start = col * size + offset + (0 if piece is None else piece * (length // 2))
        return ref.at[pl.ds(pl.multiple_of(start, 16), length if piece is None else length // 2), :]

    return part


def request_bounds(len_ref, group_ref, base, tokens):
    requests = len_ref.shape[0]
    line = lax.broadcasted_iota(jnp.int32, (requests, HD), 0)
    lane = lax.broadcasted_iota(jnp.int32, (8, HD), 1)

    def bound(r, carry):
        start, start_col, end_col, start_row, end_row, group_row = carry
        end = start + len_ref[r]
        here, there = line == r, lane == r
        return (
            end,
            jnp.where(here, start, start_col),
            jnp.where(here, end, end_col),
            jnp.where(there, start, start_row),
            jnp.where(there, end, end_row),
            jnp.where(there, group_ref[r], group_row),
        )

    column = jnp.zeros((requests, HD), jnp.int32)
    flat = jnp.full((8, HD), -1, jnp.int32)
    _, start_col, end_col, start_row, end_row, group_row = lax.fori_loop(
        0, requests, bound, (jnp.int32(0), column, column, flat, flat, flat)
    )
    start_row, end_row, group_row = start_row[0:1], end_row[0:1], group_row[0:1]
    place = base + lax.broadcasted_iota(jnp.int32, (requests, tokens), 1)
    begins = jnp.concatenate([start_col] * (tokens // HD), axis=1)
    ends = jnp.concatenate([end_col] * (tokens // HD), axis=1)
    onehot = jnp.where((begins <= place) & (place < ends), 1.0, 0.0).astype(jnp.bfloat16)
    return start_row, end_row, group_row, onehot


def project_kernel(
    owner_ref, hidden_ref, mod_ref, onehot_ref, w_ref, slot_ref, q_ref, k_ref, v_ref, near_ref, prefix_ref,
    mod_all, w_all, acc, stats, pieces, send_sem, recv_sem,
):
    at = Place()
    wire = Wire(send_sem, recv_sem)
    depth, tokens = hidden_ref.shape
    width = w_ref.shape[1]
    groups = owner_ref.shape[0]
    piece = slot_ref.shape[0] // 16
    rows = RowGather(at, wire, row_part(w_all, depth, 128), "w")
    shared = RowGather(at, wire, row_part(prefix_ref, groups * piece, groups * piece // 2), "p")
    cols = ColGather(at, wire, col_part(mod_all, depth), "m")
    row_devs = [((at.row + i) % 16, at.col) for i in range(16)]
    met = row_devs[1:] + [at.col_dev(i) for i in range(1, 16)]
    greet(met)
    w_all[pl.ds(pl.multiple_of(at.row * depth, 16), depth), :] = w_ref[...]

    hidden = hidden_ref[...].astype(jnp.float32)
    local_mean = jnp.sum(hidden, axis=0, keepdims=True) * (1.0 / depth)
    centred = hidden - local_mean
    local_square = jnp.sum(centred * centred, axis=0, keepdims=True)
    spans = tokens // 128
    mine = stats.at[at.col]
    mine[...] = jnp.zeros(mine.shape, jnp.float32)
    for j in range(spans):
        lanes = slice(128 * j, 128 * (j + 1))
        mine[j : j + 1, :] = local_mean[:, lanes]
        mine[8 + j : 9 + j, :] = local_square[:, lanes]
    meet(met)
    for i in range(1, 16):
        wire.send(("stat", i), stats.at[at.col], stats.at[at.col], at.col_dev(i))
    rows.start()

    def piece_at(ref, index):
        return ref.at[pl.ds(pl.multiple_of(index * piece, 16), piece), :]

    for i in range(1, 16):
        wire.send(("slot", i), piece_at(slot_ref, (at.row + i) % 16), piece_at(pieces, at.row), row_devs[i])
    piece_at(pieces, at.row)[...] = piece_at(slot_ref, at.row)[...]
    rows.partner()
    for i in range(1, 16):
        wire.arrived(("stat", i), stats.at[(at.col - i + 16) % 16], at.col_dev(16 - i))
    means, squares = stats[:, 0:8, :], stats[:, 8:16, :]
    mean = jnp.sum(means, axis=0) * (1.0 / 16)
    apart = means - mean[None]
    total = jnp.sum(squares, axis=0) + depth * jnp.sum(apart * apart, axis=0)
    inverse = lax.rsqrt(total * (1.0 / (16 * depth)) + 1e-06)

    def as_row(packed):
        return jnp.concatenate([packed[j : j + 1, :] for j in range(spans)], axis=1)

    onehot = onehot_ref[...]
    shift = jnp.dot(mod_ref[0], onehot, preferred_element_type=jnp.float32)
    scale = jnp.dot(mod_ref[1], onehot, preferred_element_type=jnp.float32)
    modulated = (hidden_ref[...].astype(jnp.float32) - as_row(mean)) * as_row(inverse) * (1.0 + scale) + shift
    mod_all[pl.ds(pl.multiple_of(at.col * depth, 16), depth), :] = modulated.astype(jnp.bfloat16)
    cols.start()

    for i in range(1, 16):
        wire.arrived(("slot", i), piece_at(pieces, (at.row + 16 - i) % 16), row_devs[16 - i])
    from_slot = lax.broadcasted_iota(jnp.int32, (piece, 16 * piece), 1)
    own_line = lax.broadcasted_iota(jnp.int32, (piece, 16 * piece), 0)
    for g in range(groups):
        picks = jnp.where(from_slot == owner_ref[g] * piece + own_line, 1.0, 0.0).astype(jnp.bfloat16)
        chosen = jnp.dot(picks, pieces[...], preferred_element_type=jnp.float32).astype(jnp.bfloat16)
        prefix_ref[pl.ds(pl.multiple_of((at.row * groups + g) * piece, 16), piece), :] = chosen
    shared.start()

    def product(blocks, tile):
        starts = [pl.multiple_of(at.row_at(plane, dz) * depth, 16) for plane, dz in blocks]
        lanes = pl.ds(pl.multiple_of(tile * 256, 256), 256)
        left = jnp.concatenate([mod_all[pl.ds(s, depth), lanes] for s in starts], axis=0)
        right = jnp.concatenate([w_all[pl.ds(s, depth), :] for s in starts], axis=0)
        return contract_first(left, right)

    def accumulate(blocks, fresh=False):
        def one(tile, carry):
            at_rows = pl.ds(pl.multiple_of(tile * 256, 256), 256)
            made = product(blocks, tile)
            acc[at_rows, :] = made if fresh else acc[at_rows, :] + made
            return carry

        lax.fori_loop(0, tokens // 256, one, 0)

    rows.step(1)
    cols.halves()
    cols.first(0)
    shared.partner()
    rows.step(2)
    cols.first(1)
    cols.second(0)
    shared.step(1)
    rows.step(3)
    cols.second(1)
    cols.from_core()
    shared.step(2)
    accumulate([(0, 0), (0, -1), (0, 1), (0, -2)], True)
    rows.step(4)
    shared.step(3)
    rows.from_x((0,))
    accumulate([(0, 2), (0, -3), (0, 3), (1, 0)])
    rows.from_x((-1, 1, -2, 2))
    accumulate([(1, -1), (1, 1), (1, -2), (1, 2)])
    shared.step(4)
    rows.from_x((-3, 3, -4, 4))

    heads = width // (3 * HD)
    near = near_ref.shape[0]
    own = (near - tokens) // 2
    ahead, behind = ((at.row + 1) % 16, at.col), ((at.row + 15) % 16, at.col)
    edge = own - HALO
    near_ref[0:edge, :] = jnp.zeros((edge, near_ref.shape[1]), jnp.bfloat16)
    near_ref[near - edge : near, :] = jnp.zeros((edge, near_ref.shape[1]), jnp.bfloat16)
    spans_ahead, spans_behind = [], []
    for tile in range(tokens // 256):
        low, high = tile * 256, (tile + 1) * 256
        made = (acc[low:high, :] + product([(0, 4), (1, -3), (1, 3), (1, 4)], tile)).astype(jnp.bfloat16)
        for head in range(heads):
            first = head * 3 * HD
            lanes = slice(head * HD, (head + 1) * HD)
            q_ref[low:high, lanes] = made[:, first : first + HD]
            k_ref[low:high, lanes] = made[:, first + HD : first + 2 * HD]
            v_ref[low:high, lanes] = made[:, first + 2 * HD : first + 3 * HD]
            near_ref[own + low : own + high, 2 * head * HD : 2 * (head + 1) * HD] = made[:, first + HD : first + 3 * HD]
        begin = max(low, tokens - HALO)
        spans_ahead.append((begin, high))
        wire.send(("up", tile), near_ref.at[own + begin : own + high, :], near_ref.at[begin - tokens + own : high - tokens + own, :], ahead)
        finish = min(high, HALO)
        spans_behind.append((low, finish))
        wire.send(("down", tile), near_ref.at[own + low : own + finish, :], near_ref.at[own + tokens + low : own + tokens + finish, :], behind)
    shared.from_x()
    for tile, (begin, high) in enumerate(spans_ahead):
        wire.arrived(("up", tile), near_ref.at[begin - tokens + own : high - tokens + own, :], behind)
    for tile, (low, finish) in enumerate(spans_behind):
        wire.arrived(("down", tile), near_ref.at[own + tokens + low : own + tokens + finish, :], ahead)
    wire.drain()


def project(owner, hidden_t, mod_t, onehot_t, w_qkv, slot):
    depth, tokens = hidden_t.shape
    width = w_qkv.shape[1]
    groups, slot_len = owner.shape[0], slot.shape[0]
    heads = width // (3 * HD)

    def out(rows, columns):
        return jax.ShapeDtypeStruct((rows, columns), jnp.bfloat16)

    own = out(tokens, heads * HD)
    vmem = pl.BlockSpec(memory_space=pltpu.VMEM)
    return pl.pallas_call(
        project_kernel,
        out_shape=(own, own, own, out(3 * tokens, 2 * heads * HD), out(groups * slot_len, 2 * heads * HD)),
        in_specs=[pl.BlockSpec(memory_space=pltpu.SMEM)] + [vmem] * 5,
        out_specs=(vmem,) * 5,
        scratch_shapes=[
            pltpu.VMEM((16 * depth, tokens), jnp.bfloat16),
            pltpu.VMEM((16 * depth, width), jnp.bfloat16),
            pltpu.VMEM((tokens, width), jnp.float32),
            pltpu.VMEM((16, 16, 128), jnp.float32),
            pltpu.VMEM((slot_len, 2 * heads * HD), jnp.bfloat16),
            pltpu.SemaphoreType.DMA((128,)),
            pltpu.SemaphoreType.DMA((128,)),
        ],
        compiler_params=pltpu.CompilerParams(collective_id=0, has_side_effects=True, vmem_limit_bytes=VMEM_LIMIT),
        name="project",
    )(owner, hidden_t, mod_t, onehot_t, w_qkv, slot)


def attend_kernel(
    len_ref, group_ref, mod_ref, w_out_ref, hidden_ref, q_all, near, prefix, out_ref,
    far, far_prefix, att_all, w_out_all, send_sem, recv_sem,
):
    at = Place()
    wire = Wire(send_sem, recv_sem)
    tokens = q_all.shape[0]
    heads = q_all.shape[1] // HD
    features = w_out_ref.shape[0]
    tiles = tokens // TILE
    groups = 4
    piece = prefix.shape[0] // (16 * groups)
    weights = RowGather(at, wire, row_part(w_out_all, features, features // 2), "o")
    outs = [ColGather(at, wire, col_part(att_all, tokens, t * TILE, TILE), ("a", t)) for t in range(tiles)]

    def span(start, length):
        return pl.ds(pl.multiple_of(start, 16), length)

    w_out_all[span(at.row * features, features), :] = w_out_ref[...]
    met = weights.peers() + outs[0].peers()
    greet(met)
    base = at.row * tokens
    start_row, end_row, group_row, onehot = request_bounds(len_ref, group_ref, base, tokens)
    near_len = near.shape[0]
    own = (near_len - tokens) // 2
    spot = base - own + lax.broadcasted_iota(jnp.int32, (near_len, HD), 0)
    far[...] = jnp.where((start_row <= spot) & (spot < end_row), 0.0, -BIG).astype(jnp.bfloat16)
    held = [jnp.broadcast_to(jnp.where(group_row == g, 0.0, -BIG), (piece, HD)) for g in range(groups)]
    held = jnp.concatenate(held, axis=0).astype(jnp.bfloat16)
    for r in range(16):
        far_prefix[r * groups * piece : (r + 1) * groups * piece, :] = held
    factor = math.log2(math.e) / math.sqrt(HD)
    window = TILE + 2 * (HALO + 32)

    def attend(t):
        place = base + t * TILE + lax.broadcasted_iota(jnp.int32, (TILE, HD), 0)
        belongs = jnp.where((start_row <= place) & (place < end_row), 1.0, 0.0).astype(jnp.bfloat16)
        seen = slice(own + t * TILE - HALO - 32, own + t * TILE - HALO - 32 + window)
        made = []
        hidden_from = jnp.concatenate([far_prefix[...], far[seen, :]], axis=0)
        for h in range(heads):
            lanes = slice(h * HD, (h + 1) * HD)
            of_key, of_value = slice(2 * h * HD, (2 * h + 1) * HD), slice((2 * h + 1) * HD, (2 * h + 2) * HD)
            query = jnp.concatenate([q_all[t * TILE : (t + 1) * TILE, lanes], belongs], axis=1)
            key = jnp.concatenate([jnp.concatenate([prefix[:, of_key], near[seen, of_key]], axis=0), hidden_from], axis=1)
            score = lax.dot_general(query, key, (((1,), (1,)), ((), ())), preferred_element_type=jnp.float32)
            peak = jnp.max(score, axis=1, keepdims=True) * factor
            weight = jnp.exp2(score * factor - peak)
            mass = jnp.sum(weight, axis=1, keepdims=True)
            value = jnp.concatenate([prefix[:, of_value], near[seen, of_value]], axis=0)
            summed = jnp.dot(weight.astype(jnp.bfloat16), value, preferred_element_type=jnp.float32)
            made.append((summed / mass).astype(jnp.bfloat16))
        att_all[span(at.col * tokens + t * TILE, TILE), :] = jnp.concatenate(made, axis=1)

    attend(0)
    meet(met)
    outs[0].start()
    weights.start()
    attend(1)
    outs[1].start()
    weights.partner()
    weights.step(1)
    outs[0].halves()
    outs[0].first(0)
    weights.step(2)
    attend(2)
    outs[2].start()
    outs[0].first(1)
    outs[1].halves()
    outs[1].first(0)
    weights.step(3)
    outs[0].second(0)
    outs[1].first(1)
    outs[2].halves()
    outs[0].second(1)
    outs[2].first(0)
    weights.step(4)
    outs[1].second(0)
    outs[2].first(1)
    outs[1].second(1)
    weights.from_x()
    gate = contract_first(onehot, mod_ref[2])
    right = jnp.concatenate([w_out_all[j * features : (j + 1) * features, :] for j in range(16)], axis=1)

    def finish_tile(t):
        low, high = t * TILE, (t + 1) * TILE
        outs[t].from_core()
        left = jnp.concatenate([att_all[j * tokens + low : j * tokens + high, :] for j in range(16)], axis=1)
        made = lax.dot_general(left, right, (((1,), (1,)), ((), ())), preferred_element_type=jnp.float32)
        out_ref[low:high, :] = (hidden_ref[low:high, :].astype(jnp.float32) + gate[low:high, :] * made).astype(jnp.bfloat16)

    finish_tile(0)
    outs[2].second(0)
    outs[2].second(1)
    finish_tile(1)
    finish_tile(2)
    wire.drain()


def attend(req_len, req_group, mod, w_out_t, hidden, q, near, prefix):
    tokens, own = q.shape
    features = hidden.shape[1]
    vmem = pl.BlockSpec(memory_space=pltpu.VMEM)
    return pl.pallas_call(
        attend_kernel,
        out_shape=jax.ShapeDtypeStruct(hidden.shape, jnp.bfloat16),
        in_specs=[pl.BlockSpec(memory_space=pltpu.SMEM)] * 2 + [vmem] * 6,
        out_specs=vmem,
        scratch_shapes=[
            pltpu.VMEM((near.shape[0], HD), jnp.bfloat16),
            pltpu.VMEM((prefix.shape[0], HD), jnp.bfloat16),
            pltpu.VMEM((16 * tokens, own), jnp.bfloat16),
            pltpu.VMEM((16 * features, own), jnp.bfloat16),
            pltpu.SemaphoreType.DMA((96,)),
            pltpu.SemaphoreType.DMA((96,)),
        ],
        compiler_params=pltpu.CompilerParams(collective_id=1, has_side_effects=True, vmem_limit_bytes=VMEM_LIMIT),
        name="attend",
    )(req_len, req_group, mod, w_out_t, hidden, q, near, prefix)


def shards(hidden_in, modulation, w_qkv, w_out, prefix_cache, req_group, req_len, owner):
    tokens = hidden_in.shape[0]
    requests = req_len.shape[0]
    first = lax.axis_index("row") * tokens
    earlier = jnp.arange(requests)[:, None] > jnp.arange(requests)[None, :]
    starts = jnp.sum(jnp.where(earlier, req_len[None, :], 0), axis=1)
    ends = starts + req_len
    place = first + jnp.arange(tokens, dtype=jnp.int32)
    inside = (starts[:, None] <= place[None, :]) & (place[None, :] < ends[:, None])
    onehot_t = inside.astype(jnp.bfloat16)
    mod_t = jnp.transpose(modulation[:, :2], (1, 2, 0))
    q, new_keys, new_values, near, prefix = project(
        owner, jnp.transpose(hidden_in), mod_t, onehot_t, w_qkv, prefix_cache[0]
    )
    mod = jnp.transpose(modulation, (1, 0, 2))
    hidden_out = attend(req_len, req_group, mod, jnp.transpose(w_out), hidden_in, q, near, prefix)
    return hidden_out, new_keys, new_values


def solution(mesh):
    return jax.shard_map(
        shards,
        mesh=mesh,
        in_specs=(
            P("row", "col"),
            P(None, None, "col"),
            P("row", "col"),
            P("row", "col"),
            P("row", None, "col"),
            P(),
            P(),
            P(),
        ),
        out_specs=(P("row", "col"), P("row", "col"), P("row", "col")),
        check_vma=False,
    )
```

```python
import math

import jax
import jax.numpy as jnp
from jax import lax
from jax.experimental import pallas as pl
from jax.experimental.pallas import tpu as pltpu
from jax.sharding import PartitionSpec as P

HD = 128
N_Z = 8
N_Y = 4
MESH = pl.DeviceIdType.MESH
BIG = 1e30
HALO = 672
VMEM_LIMIT = 60 << 20
TILE = 256


def contract_first(a, b):
    return lax.dot_general(a, b, (((0,), (0,)), ((), ())), preferred_element_type=jnp.float32)


class Place:
    def __init__(self):
        self.row, self.col = lax.axis_index("row"), lax.axis_index("col")
        self.l, self.z = self.row // N_Z, self.row % N_Z
        self.h, self.y, self.k = self.col // (2 * N_Y), (self.col // 2) % N_Y, self.col % 2

    def row_at(self, plane, dz):
        l = 1 - self.l if plane else self.l
        return l * N_Z + (self.z + dz + N_Z) % N_Z

    def col_at(self, half, dy, core):
        h = 1 - self.h if half else self.h
        k = 1 - self.k if core else self.k
        return (h * N_Y + (self.y + dy + N_Y) % N_Y) * 2 + k

    def z_dev(self, dz):
        return (self.row_at(0, dz), self.col)

    def x_dev(self):
        return (self.row_at(1, 0), self.col)

    def y_dev(self, dy):
        return (self.row, self.col_at(0, dy, 0))

    def half_dev(self):
        return (self.row, self.col_at(1, 0, 0))

    def core_dev(self):
        return (self.row, self.col_at(0, 0, 1))

    def col_dev(self, offset):
        return (self.row, (self.col + offset) % 16)


class Wire:
    def __init__(self, send_sem, recv_sem):
        self.send_sem, self.recv_sem = send_sem, recv_sem
        self.index, self.sent = {}, []

    def slot(self, name):
        return self.index.setdefault(name, len(self.index))

    def copy(self, name, src, dst, dev):
        n = self.slot(name)
        return pltpu.make_async_remote_copy(
            src_ref=src,
            dst_ref=dst,
            send_sem=self.send_sem.at[n],
            recv_sem=self.recv_sem.at[n],
            device_id=dev,
            device_id_type=MESH,
        )

    def send(self, name, src, dst, dev):
        c = self.copy(name, src, dst, dev)
        c.start()
        self.sent.append(c)

    def arrived(self, name, landed, dev):
        self.copy(name, landed, landed, dev).wait_recv()

    def drain(self):
        for c in self.sent:
            c.wait_send()


def greet(devices):
    barrier = pltpu.get_barrier_semaphore()
    for dev in devices:
        pl.semaphore_signal(barrier, inc=1, device_id=dev, device_id_type=MESH)


def meet(devices):
    pl.semaphore_wait(pltpu.get_barrier_semaphore(), len(devices))


class ColGather:
    def __init__(self, at, wire, part, tag):
        self.at, self.wire, self.part, self.tag = at, wire, part, tag

    def peers(self):
        at = self.at
        return [at.y_dev(1), at.y_dev(-1), at.half_dev(), at.core_dev()]

    def push(self, name, col, piece, dev):
        self.wire.send((self.tag,) + name, self.part(col, piece), self.part(col, piece), dev)

    def land(self, name, col, piece, dev):
        self.wire.arrived((self.tag,) + name, self.part(col, piece), dev)

    def start(self):
        at = self.at
        self.push(("half",), at.col, None, at.half_dev())
        for d in (1, -1):
            self.push(("y", d, 1, 0), at.col, None, at.y_dev(d))
        self.push(("core", 0, 0, None), at.col, None, at.core_dev())

    def halves(self):
        at = self.at
        block = at.col_at(1, 0, 0)
        self.land(("half",), block, None, at.half_dev())
        for d in (1, -1):
            self.push(("y", d, 1, 1), block, None, at.y_dev(d))
        self.push(("core", 1, 0, None), block, None, at.core_dev())

    def first(self, kind):
        at = self.at
        for d in (1, -1):
            block = at.col_at(kind, -d, 0)
            self.land(("y", d, 1, kind), block, None, at.y_dev(-d))
            self.push(("y", d, 2, kind), block, 0 if d == 1 else 1, at.y_dev(d))
            self.push(("core", kind, -d, None), block, None, at.core_dev())

    def second(self, kind):
        at = self.at
        for d in (1, -1):
            piece = 0 if d == 1 else 1
            block = at.col_at(kind, 2, 0)
            self.land(("y", d, 2, kind), block, piece, at.y_dev(-d))
            self.push(("core", kind, 2, piece), block, piece, at.core_dev())

    def from_core(self):
        at = self.at
        for kind, dy in ((0, 0), (1, 0), (0, -1), (0, 1), (1, -1), (1, 1), (0, 2), (1, 2)):
            for piece in (0, 1) if dy == 2 else (None,):
                self.land(("core", kind, dy, piece), at.col_at(kind, dy, 1), piece, at.core_dev())


class RowGather:
    def __init__(self, at, wire, part, tag):
        self.at, self.wire, self.part, self.tag = at, wire, part, tag

    def peers(self):
        at = self.at
        return [at.z_dev(1), at.z_dev(-1), at.x_dev()]

    def push(self, name, row, half, piece, dev):
        self.wire.send((self.tag,) + name, self.part(row, half, piece), self.part(row, half, piece), dev)

    def land(self, name, row, half, piece, dev):
        self.wire.arrived((self.tag,) + name, self.part(row, half, piece), dev)

    def start(self):
        at = self.at
        self.push(("xa",), at.row, 0, None, at.x_dev())
        for d in (1, -1):
            for kind in (0, 1):
                self.push(("z", d, 1, kind), at.row, kind, None, at.z_dev(d))
        self.push(("xb", 0, None), at.row, 1, None, at.x_dev())

    def partner(self):
        at = self.at
        block = at.row_at(1, 0)
        self.land(("xa",), block, 0, None, at.x_dev())
        for d in (1, -1):
            self.push(("z", d, 1, 2), block, 0, None, at.z_dev(d))

    def step(self, s, kinds=(0, 1, 2)):
        at = self.at
        for kind in kinds:
            half = 1 if kind == 1 else 0
            for d in (1, -1):
                block = at.row_at(1 if kind == 2 else 0, -d * s)
                side = 0 if d == 1 else 1
                piece = side if s == 4 else None
                self.land(("z", d, s, kind), block, half, piece, at.z_dev(-d))
                if s < 4:
                    self.push(("z", d, s + 1, kind), block, half, side if s == 3 else None, at.z_dev(d))
                if kind == 1:
                    self.push(("xb", -d * s, piece), block, 1, piece, at.x_dev())

    def from_x(self, offsets=(0, -1, 1, -2, 2, -3, 3, -4, 4)):
        at = self.at
        for dz in offsets:
            piece = {-4: 0, 4: 1}.get(dz)
            self.land(("xb", dz, piece), at.row_at(1, dz), 1, piece, at.x_dev())


def row_part(ref, size, crossing):
    def part(row, half, piece):
        length = size - crossing if half else crossing
        start = row * size + half * crossing
        if piece is not None:
            length = length // 2
            start = start + piece * length
        return ref.at[pl.ds(pl.multiple_of(start, 16), length), :]

    return part


def col_part(ref, size, offset=0, length=None):
    length = size if length is None else length

    def part(col, piece):
        start = col * size + offset + (0 if piece is None else piece * (length // 2))
        return ref.at[pl.ds(pl.multiple_of(start, 16), length if piece is None else length // 2), :]

    return part


def request_bounds(len_ref, group_ref, base, tokens):
    requests = len_ref.shape[0]
    line = lax.broadcasted_iota(jnp.int32, (requests, HD), 0)
    lane = lax.broadcasted_iota(jnp.int32, (8, HD), 1)

    def bound(r, carry):
        start, start_col, end_col, start_row, end_row, group_row = carry
        end = start + len_ref[r]
        here, there = line == r, lane == r
        return (
            end,
            jnp.where(here, start, start_col),
            jnp.where(here, end, end_col),
            jnp.where(there, start, start_row),
            jnp.where(there, end, end_row),
            jnp.where(there, group_ref[r], group_row),
        )

    column = jnp.zeros((requests, HD), jnp.int32)
    flat = jnp.full((8, HD), -1, jnp.int32)
    _, start_col, end_col, start_row, end_row, group_row = lax.fori_loop(
        0, requests, bound, (jnp.int32(0), column, column, flat, flat, flat)
    )
    start_row, end_row, group_row = start_row[0:1], end_row[0:1], group_row[0:1]
    place = base + lax.broadcasted_iota(jnp.int32, (requests, tokens), 1)
    begins = jnp.concatenate([start_col] * (tokens // HD), axis=1)
    ends = jnp.concatenate([end_col] * (tokens // HD), axis=1)
    onehot = jnp.where((begins <= place) & (place < ends), 1.0, 0.0).astype(jnp.bfloat16)
    return start_row, end_row, group_row, onehot


def project_kernel(
    owner_ref, hidden_ref, mod_ref, onehot_ref, w_ref, slot_ref, q_ref, k_ref, v_ref, near_ref, prefix_ref,
    mod_all, kv_all, wq_all, acc_kv, acc_q, stats, pieces, send_sem, recv_sem,
):
    at = Place()
    wire = Wire(send_sem, recv_sem)
    depth, tokens = hidden_ref.shape
    heads = w_ref.shape[1] // (3 * HD)
    groups = owner_ref.shape[0]
    piece = slot_ref.shape[0] // 16
    for_kv = RowGather(at, wire, row_part(kv_all, depth, 160), "kv")
    for_q = RowGather(at, wire, row_part(wq_all, depth, 160), "q")
    shared = RowGather(at, wire, row_part(prefix_ref, groups * piece, groups * piece // 2), "p")
    cols = ColGather(at, wire, col_part(mod_all, depth), "m")
    row_devs = [((at.row + i) % 16, at.col) for i in range(16)]
    met = row_devs[1:] + [at.col_dev(i) for i in range(1, 16)]
    greet(met)
    own_rows = pl.ds(pl.multiple_of(at.row * depth, 16), depth)
    for head in range(heads):
        first = head * 3 * HD
        wq_all[own_rows, head * HD : (head + 1) * HD] = w_ref[:, first : first + HD]
        kv_all[own_rows, 2 * head * HD : 2 * (head + 1) * HD] = w_ref[:, first + HD : first + 3 * HD]
    hidden = hidden_ref[...].astype(jnp.float32)
    local_mean = jnp.sum(hidden, axis=0, keepdims=True) * (1.0 / depth)
    centred = hidden - local_mean
    local_square = jnp.sum(centred * centred, axis=0, keepdims=True)
    spans = tokens // 128
    mine = stats.at[at.col]
    mine[...] = jnp.zeros(mine.shape, jnp.float32)
    for j in range(spans):
        lanes = slice(128 * j, 128 * (j + 1))
        mine[j : j + 1, :] = local_mean[:, lanes]
        mine[8 + j : 9 + j, :] = local_square[:, lanes]
    meet(met)
    for i in range(1, 16):
        wire.send(("stat", i), stats.at[at.col], stats.at[at.col], at.col_dev(i))
    for_kv.start()

    def piece_at(ref, index):
        return ref.at[pl.ds(pl.multiple_of(index * piece, 16), piece), :]

    for i in range(1, 16):
        wire.send(("slot", i), piece_at(slot_ref, (at.row + i) % 16), piece_at(pieces, at.row), row_devs[i])
    piece_at(pieces, at.row)[...] = piece_at(slot_ref, at.row)[...]
    for_kv.partner()
    for i in range(1, 16):
        wire.arrived(("stat", i), stats.at[(at.col - i + 16) % 16], at.col_dev(16 - i))
    means, squares = stats[:, 0:8, :], stats[:, 8:16, :]
    mean = jnp.sum(means, axis=0) * (1.0 / 16)
    apart = means - mean[None]
    total = jnp.sum(squares, axis=0) + depth * jnp.sum(apart * apart, axis=0)
    inverse = lax.rsqrt(total * (1.0 / (16 * depth)) + 1e-06)

    def as_row(packed):
        return jnp.concatenate([packed[j : j + 1, :] for j in range(spans)], axis=1)

    onehot = onehot_ref[...]
    shift = contract_first(mod_ref[0], onehot)
    scale = contract_first(mod_ref[1], onehot)
    modulated = (hidden_ref[...].astype(jnp.float32) - as_row(mean)) * as_row(inverse) * (1.0 + scale) + shift
    mod_all[pl.ds(pl.multiple_of(at.col * depth, 16), depth), :] = modulated.astype(jnp.bfloat16)
    cols.start()

    for i in range(1, 16):
        wire.arrived(("slot", i), piece_at(pieces, (at.row + 16 - i) % 16), row_devs[16 - i])
    from_slot = lax.broadcasted_iota(jnp.int32, (piece, 16 * piece), 1)
    own_line = lax.broadcasted_iota(jnp.int32, (piece, 16 * piece), 0)
    for g in range(groups):
        picks = jnp.where(from_slot == owner_ref[g] * piece + own_line, 1.0, 0.0).astype(jnp.bfloat16)
        chosen = jnp.dot(picks, pieces[...], preferred_element_type=jnp.float32).astype(jnp.bfloat16)
        prefix_ref[pl.ds(pl.multiple_of((at.row * groups + g) * piece, 16), piece), :] = chosen

    def product(weight, blocks, tile):
        starts = [pl.multiple_of(at.row_at(plane, dz) * depth, 16) for plane, dz in blocks]
        lanes = pl.ds(pl.multiple_of(tile * 256, 256), 256)
        left = jnp.concatenate([mod_all[pl.ds(s, depth), lanes] for s in starts], axis=0)
        right = jnp.concatenate([weight[pl.ds(s, depth), :] for s in starts], axis=0)
        return contract_first(left, right)

    def accumulate(acc, weight, blocks, fresh=False):
        def one(tile, carry):
            at_rows = pl.ds(pl.multiple_of(tile * 256, 256), 256)
            made = product(weight, blocks, tile)
            acc[at_rows, :] = made if fresh else acc[at_rows, :] + made
            return carry

        lax.fori_loop(0, tokens // 256, one, 0)

    quarters = (
        [(0, 0), (0, -1), (0, 1), (0, -2)],
        [(0, 2), (0, -3), (0, 3), (1, 0)],
        [(1, -1), (1, 1), (1, -2), (1, 2)],
        [(0, 4), (1, -3), (1, 3), (1, 4)],
    )
    for_kv.step(1)
    cols.halves()
    cols.first(0)
    for_kv.step(2)
    cols.first(1)
    cols.second(0)
    for_kv.step(3)
    for_q.start()
    cols.second(1)
    for_kv.step(4)
    for_q.partner()
    for_kv.from_x((0, -1, 1))
    shared.start()
    cols.from_core()
    accumulate(acc_kv, kv_all, quarters[0], True)
    for_q.step(1)
    shared.partner()
    accumulate(acc_kv, kv_all, quarters[1])
    for_kv.from_x((-2, 2))
    accumulate(acc_kv, kv_all, quarters[2])
    for_kv.from_x((-3, 3, -4, 4))

    near = near_ref.shape[0]
    own = (near - tokens) // 2
    ahead, behind = ((at.row + 1) % 16, at.col), ((at.row + 15) % 16, at.col)
    edge = own - HALO
    near_ref[0:edge, :] = jnp.zeros((edge, near_ref.shape[1]), jnp.bfloat16)
    near_ref[near - edge : near, :] = jnp.zeros((edge, near_ref.shape[1]), jnp.bfloat16)
    spans_ahead, spans_behind = [], []
    for tile in range(tokens // 256):
        low, high = tile * 256, (tile + 1) * 256
        made = (acc_kv[low:high, :] + product(kv_all, quarters[3], tile)).astype(jnp.bfloat16)
        near_ref[own + low : own + high, :] = made
        for head in range(heads):
            lanes = slice(head * HD, (head + 1) * HD)
            k_ref[low:high, lanes] = made[:, 2 * head * HD : (2 * head + 1) * HD]
            v_ref[low:high, lanes] = made[:, (2 * head + 1) * HD : (2 * head + 2) * HD]
        begin = max(low, tokens - HALO)
        spans_ahead.append((begin, high))
        wire.send(("up", tile), near_ref.at[own + begin : own + high, :], near_ref.at[begin - tokens + own : high - tokens + own, :], ahead)
        finish = min(high, HALO)
        spans_behind.append((low, finish))
        wire.send(("down", tile), near_ref.at[own + low : own + finish, :], near_ref.at[own + tokens + low : own + tokens + finish, :], behind)
    for_q.step(2)
    shared.step(1)
    accumulate(acc_q, wq_all, quarters[0], True)
    for_q.step(3)
    shared.step(2)
    for_q.from_x((0,))
    accumulate(acc_q, wq_all, quarters[1])
    for_q.step(4)
    shared.step(3)
    for_q.from_x((-1, 1, -2, 2))
    accumulate(acc_q, wq_all, quarters[2])
    shared.step(4)
    for_q.from_x((-3, 3, -4, 4))
    for tile in range(tokens // 256):
        low, high = tile * 256, (tile + 1) * 256
        q_ref[low:high, :] = (acc_q[low:high, :] + product(wq_all, quarters[3], tile)).astype(jnp.bfloat16)
    shared.from_x()
    for tile, (begin, high) in enumerate(spans_ahead):
        wire.arrived(("up", tile), near_ref.at[begin - tokens + own : high - tokens + own, :], behind)
    for tile, (low, finish) in enumerate(spans_behind):
        wire.arrived(("down", tile), near_ref.at[own + tokens + low : own + tokens + finish, :], ahead)
    wire.drain()


def project(owner, hidden_t, mod, onehot_t, w_qkv, slot):
    depth, tokens = hidden_t.shape
    width = w_qkv.shape[1]
    groups, slot_len = owner.shape[0], slot.shape[0]
    heads = width // (3 * HD)

    def out(rows, columns):
        return jax.ShapeDtypeStruct((rows, columns), jnp.bfloat16)

    own = out(tokens, heads * HD)
    vmem = pl.BlockSpec(memory_space=pltpu.VMEM)
    return pl.pallas_call(
        project_kernel,
        out_shape=(own, own, own, out(3 * tokens, 2 * heads * HD), out(groups * slot_len, 2 * heads * HD)),
        in_specs=[pl.BlockSpec(memory_space=pltpu.SMEM)] + [vmem] * 5,
        out_specs=(vmem,) * 5,
        scratch_shapes=[
            pltpu.VMEM((16 * depth, tokens), jnp.bfloat16),
            pltpu.VMEM((16 * depth, 2 * heads * HD), jnp.bfloat16),
            pltpu.VMEM((16 * depth, heads * HD), jnp.bfloat16),
            pltpu.VMEM((tokens, 2 * heads * HD), jnp.float32),
            pltpu.VMEM((tokens, heads * HD), jnp.float32),
            pltpu.VMEM((16, 16, 128), jnp.float32),
            pltpu.VMEM((slot_len, 2 * heads * HD), jnp.bfloat16),
            pltpu.SemaphoreType.DMA((160,)),
            pltpu.SemaphoreType.DMA((160,)),
        ],
        compiler_params=pltpu.CompilerParams(collective_id=0, has_side_effects=True, vmem_limit_bytes=VMEM_LIMIT),
        name="project",
    )(owner, hidden_t, mod, onehot_t, w_qkv, slot)


def attend_kernel(
    len_ref, group_ref, mod_ref, w_out_ref, hidden_ref, q_all, near, prefix, out_ref,
    far, far_prefix, att_all, w_out_all, send_sem, recv_sem,
):
    at = Place()
    wire = Wire(send_sem, recv_sem)
    tokens = q_all.shape[0]
    heads = q_all.shape[1] // HD
    features = w_out_ref.shape[0]
    tiles = tokens // TILE
    groups = 4
    piece = prefix.shape[0] // (16 * groups)
    weights = RowGather(at, wire, row_part(w_out_all, features, features // 2), "o")
    outs = [ColGather(at, wire, col_part(att_all, tokens, t * TILE, TILE), ("a", t)) for t in range(tiles)]

    def span(start, length):
        return pl.ds(pl.multiple_of(start, 16), length)

    w_out_all[span(at.row * features, features), :] = w_out_ref[...]
    met = weights.peers() + outs[0].peers()
    greet(met)
    base = at.row * tokens
    start_row, end_row, group_row, onehot = request_bounds(len_ref, group_ref, base, tokens)
    near_len = near.shape[0]
    own = (near_len - tokens) // 2
    spot = base - own + lax.broadcasted_iota(jnp.int32, (near_len, HD), 0)
    far[...] = jnp.where((start_row <= spot) & (spot < end_row), 0.0, -BIG).astype(jnp.bfloat16)
    held = [jnp.broadcast_to(jnp.where(group_row == g, 0.0, -BIG), (piece, HD)) for g in range(groups)]
    held = jnp.concatenate(held, axis=0).astype(jnp.bfloat16)
    for r in range(16):
        far_prefix[r * groups * piece : (r + 1) * groups * piece, :] = held
    factor = math.log2(math.e) / math.sqrt(HD)
    window = TILE + 2 * (HALO + 32)

    def attend(t):
        place = base + t * TILE + lax.broadcasted_iota(jnp.int32, (TILE, HD), 0)
        belongs = jnp.where((start_row <= place) & (place < end_row), 1.0, 0.0).astype(jnp.bfloat16)
        seen = slice(own + t * TILE - HALO - 32, own + t * TILE - HALO - 32 + window)
        made = []
        hidden_from = jnp.concatenate([far_prefix[...], far[seen, :]], axis=0)
        for h in range(heads):
            lanes = slice(h * HD, (h + 1) * HD)
            of_key, of_value = slice(2 * h * HD, (2 * h + 1) * HD), slice((2 * h + 1) * HD, (2 * h + 2) * HD)
            query = jnp.concatenate([q_all[t * TILE : (t + 1) * TILE, lanes], belongs], axis=1)
            key = jnp.concatenate([jnp.concatenate([prefix[:, of_key], near[seen, of_key]], axis=0), hidden_from], axis=1)
            score = lax.dot_general(query, key, (((1,), (1,)), ((), ())), preferred_element_type=jnp.float32)
            peak = jnp.max(score, axis=1, keepdims=True) * factor
            weight = jnp.exp2(score * factor - peak)
            mass = jnp.sum(weight, axis=1, keepdims=True)
            value = jnp.concatenate([prefix[:, of_value], near[seen, of_value]], axis=0)
            summed = jnp.dot(weight.astype(jnp.bfloat16), value, preferred_element_type=jnp.float32)
            made.append((summed / mass).astype(jnp.bfloat16))
        att_all[span(at.col * tokens + t * TILE, TILE), :] = jnp.concatenate(made, axis=1)

    attend(0)
    meet(met)
    outs[0].start()
    weights.start()
    attend(1)
    outs[1].start()
    weights.partner()
    weights.step(1)
    outs[0].halves()
    outs[0].first(0)
    weights.step(2)
    attend(2)
    outs[2].start()
    outs[0].first(1)
    outs[1].halves()
    outs[1].first(0)
    weights.step(3)
    outs[0].second(0)
    outs[1].first(1)
    outs[2].halves()
    outs[0].second(1)
    outs[2].first(0)
    weights.step(4)
    outs[1].second(0)
    outs[2].first(1)
    outs[1].second(1)
    weights.from_x()
    gate = contract_first(mod_ref[2], onehot)
    right = jnp.concatenate([w_out_all[j * features : (j + 1) * features, :] for j in range(16)], axis=1)

    def finish_tile(t):
        low, high = t * TILE, (t + 1) * TILE
        outs[t].from_core()
        left = jnp.concatenate([att_all[j * tokens + low : j * tokens + high, :] for j in range(16)], axis=1)
        made = lax.dot_general(right, left, (((1,), (1,)), ((), ())), preferred_element_type=jnp.float32)
        out_ref[:, low:high] = (hidden_ref[:, low:high].astype(jnp.float32) + gate[:, low:high] * made).astype(jnp.bfloat16)

    finish_tile(0)
    outs[2].second(0)
    outs[2].second(1)
    finish_tile(1)
    finish_tile(2)
    wire.drain()


def attend(req_len, req_group, mod, w_out_t, hidden, q, near, prefix):
    tokens, own = q.shape
    features = hidden.shape[0]
    vmem = pl.BlockSpec(memory_space=pltpu.VMEM)
    return pl.pallas_call(
        attend_kernel,
        out_shape=jax.ShapeDtypeStruct(hidden.shape, jnp.bfloat16),
        in_specs=[pl.BlockSpec(memory_space=pltpu.SMEM)] * 2 + [vmem] * 6,
        out_specs=vmem,
        scratch_shapes=[
            pltpu.VMEM((near.shape[0], HD), jnp.bfloat16),
            pltpu.VMEM((prefix.shape[0], HD), jnp.bfloat16),
            pltpu.VMEM((16 * tokens, own), jnp.bfloat16),
            pltpu.VMEM((16 * features, own), jnp.bfloat16),
            pltpu.SemaphoreType.DMA((96,)),
            pltpu.SemaphoreType.DMA((96,)),
        ],
        compiler_params=pltpu.CompilerParams(collective_id=1, has_side_effects=True, vmem_limit_bytes=VMEM_LIMIT),
        name="attend",
    )(req_len, req_group, mod, w_out_t, hidden, q, near, prefix)


def shards(hidden_in, modulation, w_qkv, w_out, prefix_cache, req_group, req_len, owner):
    tokens = hidden_in.shape[0]
    requests = req_len.shape[0]
    first = lax.axis_index("row") * tokens
    earlier = jnp.arange(requests)[:, None] > jnp.arange(requests)[None, :]
    starts = jnp.sum(jnp.where(earlier, req_len[None, :], 0), axis=1)
    ends = starts + req_len
    place = first + jnp.arange(tokens, dtype=jnp.int32)
    inside = (starts[:, None] <= place[None, :]) & (place[None, :] < ends[:, None])
    onehot_t = inside.astype(jnp.bfloat16)
    mod = jnp.transpose(modulation, (1, 0, 2))
    hidden_t = jnp.transpose(hidden_in)
    q, new_keys, new_values, near, prefix = project(
        owner, hidden_t, mod, onehot_t, w_qkv, prefix_cache[0]
    )
    hidden_out = attend(req_len, req_group, mod, jnp.transpose(w_out), hidden_t, q, near, prefix)
    return jnp.transpose(hidden_out), new_keys, new_values


def solution(mesh):
    return jax.shard_map(
        shards,
        mesh=mesh,
        in_specs=(
            P("row", "col"),
            P(None, None, "col"),
            P("row", "col"),
            P("row", "col"),
            P("row", None, "col"),
            P(),
            P(),
            P(),
        ),
        out_specs=(P("row", "col"), P("row", "col"), P("row", "col")),
        check_vma=False,
    )
```

```python
import math

import jax
import jax.numpy as jnp
from jax import lax
from jax.experimental import pallas as pl
from jax.experimental.pallas import tpu as pltpu
from jax.sharding import PartitionSpec as P

HD = 128
N_Z = 8
N_Y = 4
MESH = pl.DeviceIdType.MESH
BIG = 1e30
HALO = 672
VMEM_LIMIT = 60 << 20
TILE = 256


def contract_first(a, b):
    return lax.dot_general(a, b, (((0,), (0,)), ((), ())), preferred_element_type=jnp.float32)


class Place:
    def __init__(self):
        self.row, self.col = lax.axis_index("row"), lax.axis_index("col")
        self.l, self.z = self.row // N_Z, self.row % N_Z
        self.h, self.y, self.k = self.col // (2 * N_Y), (self.col // 2) % N_Y, self.col % 2

    def row_at(self, plane, dz):
        l = 1 - self.l if plane else self.l
        return l * N_Z + (self.z + dz + N_Z) % N_Z

    def col_at(self, half, dy, core):
        h = 1 - self.h if half else self.h
        k = 1 - self.k if core else self.k
        return (h * N_Y + (self.y + dy + N_Y) % N_Y) * 2 + k

    def z_dev(self, dz):
        return (self.row_at(0, dz), self.col)

    def x_dev(self):
        return (self.row_at(1, 0), self.col)

    def y_dev(self, dy):
        return (self.row, self.col_at(0, dy, 0))

    def half_dev(self):
        return (self.row, self.col_at(1, 0, 0))

    def core_dev(self):
        return (self.row, self.col_at(0, 0, 1))

    def col_dev(self, offset):
        return (self.row, (self.col + offset) % 16)


class Wire:
    def __init__(self, send_sem, recv_sem):
        self.send_sem, self.recv_sem = send_sem, recv_sem
        self.index, self.sent = {}, []

    def slot(self, name):
        return self.index.setdefault(name, len(self.index))

    def copy(self, name, src, dst, dev):
        n = self.slot(name)
        return pltpu.make_async_remote_copy(
            src_ref=src,
            dst_ref=dst,
            send_sem=self.send_sem.at[n],
            recv_sem=self.recv_sem.at[n],
            device_id=dev,
            device_id_type=MESH,
        )

    def send(self, name, src, dst, dev):
        c = self.copy(name, src, dst, dev)
        c.start()
        self.sent.append(c)

    def arrived(self, name, landed, dev):
        self.copy(name, landed, landed, dev).wait_recv()

    def drain(self):
        for c in self.sent:
            c.wait_send()


def greet(devices):
    barrier = pltpu.get_barrier_semaphore()
    for dev in devices:
        pl.semaphore_signal(barrier, inc=1, device_id=dev, device_id_type=MESH)


def meet(devices):
    pl.semaphore_wait(pltpu.get_barrier_semaphore(), len(devices))


class ColGather:
    def __init__(self, at, wire, part, tag):
        self.at, self.wire, self.part, self.tag = at, wire, part, tag

    def peers(self):
        at = self.at
        return [at.y_dev(1), at.y_dev(-1), at.half_dev(), at.core_dev()]

    def push(self, name, col, piece, dev):
        self.wire.send((self.tag,) + name, self.part(col, piece), self.part(col, piece), dev)

    def land(self, name, col, piece, dev):
        self.wire.arrived((self.tag,) + name, self.part(col, piece), dev)

    def start(self):
        at = self.at
        self.push(("half",), at.col, None, at.half_dev())
        for d in (1, -1):
            self.push(("y", d, 1, 0), at.col, None, at.y_dev(d))
        self.push(("core", 0, 0, None), at.col, None, at.core_dev())

    def halves(self):
        at = self.at
        block = at.col_at(1, 0, 0)
        self.land(("half",), block, None, at.half_dev())
        for d in (1, -1):
            self.push(("y", d, 1, 1), block, None, at.y_dev(d))
        self.push(("core", 1, 0, None), block, None, at.core_dev())

    def first(self, kind):
        at = self.at
        for d in (1, -1):
            block = at.col_at(kind, -d, 0)
            self.land(("y", d, 1, kind), block, None, at.y_dev(-d))
            self.push(("y", d, 2, kind), block, 0 if d == 1 else 1, at.y_dev(d))
            self.push(("core", kind, -d, None), block, None, at.core_dev())

    def second(self, kind):
        at = self.at
        for d in (1, -1):
            piece = 0 if d == 1 else 1
            block = at.col_at(kind, 2, 0)
            self.land(("y", d, 2, kind), block, piece, at.y_dev(-d))
            self.push(("core", kind, 2, piece), block, piece, at.core_dev())

    def from_core(self):
        at = self.at
        for kind, dy in ((0, 0), (1, 0), (0, -1), (0, 1), (1, -1), (1, 1), (0, 2), (1, 2)):
            for piece in (0, 1) if dy == 2 else (None,):
                self.land(("core", kind, dy, piece), at.col_at(kind, dy, 1), piece, at.core_dev())


class RowGather:
    def __init__(self, at, wire, part, tag):
        self.at, self.wire, self.part, self.tag = at, wire, part, tag

    def peers(self):
        at = self.at
        return [at.z_dev(1), at.z_dev(-1), at.x_dev()]

    def push(self, name, row, half, piece, dev):
        self.wire.send((self.tag,) + name, self.part(row, half, piece), self.part(row, half, piece), dev)

    def land(self, name, row, half, piece, dev):
        self.wire.arrived((self.tag,) + name, self.part(row, half, piece), dev)

    def start(self):
        at = self.at
        self.push(("xa",), at.row, 0, None, at.x_dev())
        for d in (1, -1):
            for kind in (0, 1):
                self.push(("z", d, 1, kind), at.row, kind, None, at.z_dev(d))
        self.push(("xb", 0, None), at.row, 1, None, at.x_dev())

    def partner(self):
        at = self.at
        block = at.row_at(1, 0)
        self.land(("xa",), block, 0, None, at.x_dev())
        for d in (1, -1):
            self.push(("z", d, 1, 2), block, 0, None, at.z_dev(d))

    def step(self, s, kinds=(0, 1, 2)):
        at = self.at
        for kind in kinds:
            half = 1 if kind == 1 else 0
            for d in (1, -1):
                block = at.row_at(1 if kind == 2 else 0, -d * s)
                side = 0 if d == 1 else 1
                piece = side if s == 4 else None
                self.land(("z", d, s, kind), block, half, piece, at.z_dev(-d))
                if s < 4:
                    self.push(("z", d, s + 1, kind), block, half, side if s == 3 else None, at.z_dev(d))
                if kind == 1:
                    self.push(("xb", -d * s, piece), block, 1, piece, at.x_dev())

    def from_x(self, offsets=(0, -1, 1, -2, 2, -3, 3, -4, 4)):
        at = self.at
        for dz in offsets:
            piece = {-4: 0, 4: 1}.get(dz)
            self.land(("xb", dz, piece), at.row_at(1, dz), 1, piece, at.x_dev())


def row_part(ref, size, crossing):
    def part(row, half, piece):
        length = size - crossing if half else crossing
        start = row * size + half * crossing
        if piece is not None:
            length = length // 2
            start = start + piece * length
        return ref.at[pl.ds(pl.multiple_of(start, 16), length), :]

    return part


def col_part(ref, size, offset=0, length=None):
    length = size if length is None else length

    def part(col, piece):
        start = col * size + offset + (0 if piece is None else piece * (length // 2))
        return ref.at[pl.ds(pl.multiple_of(start, 16), length if piece is None else length // 2), :]

    return part


def request_bounds(len_ref, group_ref, base, tokens):
    requests = len_ref.shape[0]
    line = lax.broadcasted_iota(jnp.int32, (requests, HD), 0)
    lane = lax.broadcasted_iota(jnp.int32, (8, HD), 1)

    def bound(r, carry):
        start, start_col, end_col, start_row, end_row, group_row = carry
        end = start + len_ref[r]
        here, there = line == r, lane == r
        return (
            end,
            jnp.where(here, start, start_col),
            jnp.where(here, end, end_col),
            jnp.where(there, start, start_row),
            jnp.where(there, end, end_row),
            jnp.where(there, group_ref[r], group_row),
        )

    column = jnp.zeros((requests, HD), jnp.int32)
    flat = jnp.full((8, HD), -1, jnp.int32)
    _, start_col, end_col, start_row, end_row, group_row = lax.fori_loop(
        0, requests, bound, (jnp.int32(0), column, column, flat, flat, flat)
    )
    start_row, end_row, group_row = start_row[0:1], end_row[0:1], group_row[0:1]
    place = base + lax.broadcasted_iota(jnp.int32, (requests, tokens), 1)
    begins = jnp.concatenate([start_col] * (tokens // HD), axis=1)
    ends = jnp.concatenate([end_col] * (tokens // HD), axis=1)
    onehot = jnp.where((begins <= place) & (place < ends), 1.0, 0.0).astype(jnp.bfloat16)
    return start_row, end_row, group_row, onehot


def project_kernel(
    owner_ref, hidden_ref, mod_ref, onehot_ref, w_ref, slot_ref, q_ref, k_ref, v_ref, near_ref, prefix_ref,
    mod_all, kv_all, wq_all, acc_kv, acc_q, stats, pieces, send_sem, recv_sem,
):
    at = Place()
    wire = Wire(send_sem, recv_sem)
    depth, tokens = hidden_ref.shape
    heads = w_ref.shape[1] // (3 * HD)
    groups = owner_ref.shape[0]
    piece = slot_ref.shape[0] // 16
    for_kv = RowGather(at, wire, row_part(kv_all, depth, 160), "kv")
    for_q = RowGather(at, wire, row_part(wq_all, depth, 160), "q")
    shared = RowGather(at, wire, row_part(prefix_ref, groups * piece, groups * piece // 2), "p")
    cols = ColGather(at, wire, col_part(mod_all, depth), "m")
    row_devs = [((at.row + i) % 16, at.col) for i in range(16)]
    met = row_devs[1:] + [at.col_dev(i) for i in range(1, 16)]
    greet(met)
    own_rows = pl.ds(pl.multiple_of(at.row * depth, 16), depth)
    for head in range(heads):
        first = head * 3 * HD
        wq_all[own_rows, head * HD : (head + 1) * HD] = w_ref[:, first : first + HD]
        kv_all[own_rows, 2 * head * HD : 2 * (head + 1) * HD] = w_ref[:, first + HD : first + 3 * HD]
    hidden = hidden_ref[...].astype(jnp.float32)
    local_mean = jnp.sum(hidden, axis=0, keepdims=True) * (1.0 / depth)
    centred = hidden - local_mean
    local_square = jnp.sum(centred * centred, axis=0, keepdims=True)
    spans = tokens // 128
    mine = stats.at[at.col]
    mine[...] = jnp.zeros(mine.shape, jnp.float32)
    for j in range(spans):
        lanes = slice(128 * j, 128 * (j + 1))
        mine[j : j + 1, :] = local_mean[:, lanes]
        mine[8 + j : 9 + j, :] = local_square[:, lanes]
    meet(met)
    for i in range(1, 16):
        wire.send(("stat", i), stats.at[at.col], stats.at[at.col], at.col_dev(i))
    for_kv.start()

    def piece_at(ref, index):
        return ref.at[pl.ds(pl.multiple_of(index * piece, 16), piece), :]

    for i in range(1, 16):
        wire.send(("slot", i), piece_at(slot_ref, (at.row + i) % 16), piece_at(pieces, at.row), row_devs[i])
    piece_at(pieces, at.row)[...] = piece_at(slot_ref, at.row)[...]
    for_kv.partner()
    for i in range(1, 16):
        wire.arrived(("stat", i), stats.at[(at.col - i + 16) % 16], at.col_dev(16 - i))
    means, squares = stats[:, 0:8, :], stats[:, 8:16, :]
    mean = jnp.sum(means, axis=0) * (1.0 / 16)
    apart = means - mean[None]
    total = jnp.sum(squares, axis=0) + depth * jnp.sum(apart * apart, axis=0)
    inverse = lax.rsqrt(total * (1.0 / (16 * depth)) + 1e-06)

    def as_row(packed):
        return jnp.concatenate([packed[j : j + 1, :] for j in range(spans)], axis=1)

    onehot = onehot_ref[...]
    shift = contract_first(mod_ref[0], onehot)
    scale = contract_first(mod_ref[1], onehot)
    modulated = (hidden_ref[...].astype(jnp.float32) - as_row(mean)) * as_row(inverse) * (1.0 + scale) + shift
    mod_all[pl.ds(pl.multiple_of(at.col * depth, 16), depth), :] = modulated.astype(jnp.bfloat16)
    cols.start()

    for i in range(1, 16):
        wire.arrived(("slot", i), piece_at(pieces, (at.row + 16 - i) % 16), row_devs[16 - i])
    from_slot = lax.broadcasted_iota(jnp.int32, (piece, 16 * piece), 1)
    own_line = lax.broadcasted_iota(jnp.int32, (piece, 16 * piece), 0)
    for g in range(groups):
        picks = jnp.where(from_slot == owner_ref[g] * piece + own_line, 1.0, 0.0).astype(jnp.bfloat16)
        chosen = jnp.dot(picks, pieces[...], preferred_element_type=jnp.float32).astype(jnp.bfloat16)
        prefix_ref[pl.ds(pl.multiple_of((at.row * groups + g) * piece, 16), piece), :] = chosen

    def product(weight, blocks, tile):
        starts = [pl.multiple_of(at.row_at(plane, dz) * depth, 16) for plane, dz in blocks]
        lanes = pl.ds(pl.multiple_of(tile * 256, 256), 256)
        left = jnp.concatenate([mod_all[pl.ds(s, depth), lanes] for s in starts], axis=0)
        right = jnp.concatenate([weight[pl.ds(s, depth), :] for s in starts], axis=0)
        return contract_first(left, right)

    def accumulate(acc, weight, blocks, fresh=False):
        def one(tile, carry):
            at_rows = pl.ds(pl.multiple_of(tile * 256, 256), 256)
            made = product(weight, blocks, tile)
            acc[at_rows, :] = made if fresh else acc[at_rows, :] + made
            return carry

        lax.fori_loop(0, tokens // 256, one, 0)

    quarters = (
        [(0, 0), (0, -1), (0, 1), (0, -2)],
        [(0, 2), (0, -3), (0, 3), (1, 0)],
        [(1, -1), (1, 1), (1, -2), (1, 2)],
        [(0, 4), (1, -3), (1, 3), (1, 4)],
    )
    for_kv.step(1)
    cols.halves()
    cols.first(0)
    for_kv.step(2)
    cols.first(1)
    cols.second(0)
    for_kv.step(3)
    for_q.start()
    cols.second(1)
    for_kv.step(4)
    for_q.partner()
    for_kv.from_x((0, -1, 1))
    shared.start()
    cols.from_core()
    accumulate(acc_kv, kv_all, quarters[0], True)
    for_q.step(1)
    shared.partner()
    accumulate(acc_kv, kv_all, quarters[1])
    for_kv.from_x((-2, 2))
    accumulate(acc_kv, kv_all, quarters[2])
    for_kv.from_x((-3, 3, -4, 4))

    near = near_ref.shape[0]
    own = (near - tokens) // 2
    ahead, behind = ((at.row + 1) % 16, at.col), ((at.row + 15) % 16, at.col)
    edge = own - HALO
    near_ref[0:edge, :] = jnp.zeros((edge, near_ref.shape[1]), jnp.bfloat16)
    near_ref[near - edge : near, :] = jnp.zeros((edge, near_ref.shape[1]), jnp.bfloat16)
    spans_ahead, spans_behind = [], []
    for tile in range(tokens // 256):
        low, high = tile * 256, (tile + 1) * 256
        made = (acc_kv[low:high, :] + product(kv_all, quarters[3], tile)).astype(jnp.bfloat16)
        near_ref[own + low : own + high, :] = made
        for head in range(heads):
            lanes = slice(head * HD, (head + 1) * HD)
            k_ref[low:high, lanes] = made[:, 2 * head * HD : (2 * head + 1) * HD]
            v_ref[low:high, lanes] = made[:, (2 * head + 1) * HD : (2 * head + 2) * HD]
        begin = max(low, tokens - HALO)
        spans_ahead.append((begin, high))
        wire.send(("up", tile), near_ref.at[own + begin : own + high, :], near_ref.at[begin - tokens + own : high - tokens + own, :], ahead)
        finish = min(high, HALO)
        spans_behind.append((low, finish))
        wire.send(("down", tile), near_ref.at[own + low : own + finish, :], near_ref.at[own + tokens + low : own + tokens + finish, :], behind)
    for_q.step(2)
    shared.step(1)
    accumulate(acc_q, wq_all, quarters[0], True)
    for_q.step(3)
    shared.step(2)
    for_q.from_x((0,))
    accumulate(acc_q, wq_all, quarters[1])
    for_q.step(4)
    shared.step(3)
    for_q.from_x((-1, 1, -2, 2))
    accumulate(acc_q, wq_all, quarters[2])
    shared.step(4)
    for_q.from_x((-3, 3, -4, 4))
    for tile in range(tokens // 256):
        low, high = tile * 256, (tile + 1) * 256
        q_ref[low:high, :] = (acc_q[low:high, :] + product(wq_all, quarters[3], tile)).astype(jnp.bfloat16)
    shared.from_x()
    for tile, (begin, high) in enumerate(spans_ahead):
        wire.arrived(("up", tile), near_ref.at[begin - tokens + own : high - tokens + own, :], behind)
    for tile, (low, finish) in enumerate(spans_behind):
        wire.arrived(("down", tile), near_ref.at[own + tokens + low : own + tokens + finish, :], ahead)
    wire.drain()


def project(owner, hidden_t, mod, onehot_t, w_qkv, slot):
    depth, tokens = hidden_t.shape
    width = w_qkv.shape[1]
    groups, slot_len = owner.shape[0], slot.shape[0]
    heads = width // (3 * HD)

    def out(rows, columns):
        return jax.ShapeDtypeStruct((rows, columns), jnp.bfloat16)

    own = out(tokens, heads * HD)
    vmem = pl.BlockSpec(memory_space=pltpu.VMEM)
    return pl.pallas_call(
        project_kernel,
        out_shape=(own, own, own, out(3 * tokens, 2 * heads * HD), out(groups * slot_len, 2 * heads * HD)),
        in_specs=[pl.BlockSpec(memory_space=pltpu.SMEM)] + [vmem] * 5,
        out_specs=(vmem,) * 5,
        scratch_shapes=[
            pltpu.VMEM((16 * depth, tokens), jnp.bfloat16),
            pltpu.VMEM((16 * depth, 2 * heads * HD), jnp.bfloat16),
            pltpu.VMEM((16 * depth, heads * HD), jnp.bfloat16),
            pltpu.VMEM((tokens, 2 * heads * HD), jnp.float32),
            pltpu.VMEM((tokens, heads * HD), jnp.float32),
            pltpu.VMEM((16, 16, 128), jnp.float32),
            pltpu.VMEM((slot_len, 2 * heads * HD), jnp.bfloat16),
            pltpu.SemaphoreType.DMA((160,)),
            pltpu.SemaphoreType.DMA((160,)),
        ],
        compiler_params=pltpu.CompilerParams(collective_id=0, has_side_effects=True, vmem_limit_bytes=VMEM_LIMIT),
        name="project",
    )(owner, hidden_t, mod, onehot_t, w_qkv, slot)


def attend_kernel(
    len_ref, group_ref, mod_ref, w_out_ref, hidden_ref, q_all, near, prefix, out_ref,
    far, far_prefix, att_all, w_out_all, send_sem, recv_sem,
):
    at = Place()
    wire = Wire(send_sem, recv_sem)
    tokens = q_all.shape[0]
    heads = q_all.shape[1] // HD
    features = w_out_ref.shape[0]
    tiles = tokens // TILE
    groups = 4
    piece = prefix.shape[0] // (16 * groups)
    weights = RowGather(at, wire, row_part(w_out_all, features, features // 2), "o")
    outs = [ColGather(at, wire, col_part(att_all, tokens, t * TILE, TILE), ("a", t)) for t in range(tiles)]

    def span(start, length):
        return pl.ds(pl.multiple_of(start, 16), length)

    w_out_all[span(at.row * features, features), :] = w_out_ref[...]
    met = weights.peers() + outs[0].peers()
    greet(met)
    base = at.row * tokens
    start_row, end_row, group_row, onehot = request_bounds(len_ref, group_ref, base, tokens)
    near_len = near.shape[0]
    own = (near_len - tokens) // 2
    spot = base - own + lax.broadcasted_iota(jnp.int32, (near_len, HD), 0)
    far[...] = jnp.where((start_row <= spot) & (spot < end_row), 0.0, -BIG).astype(jnp.bfloat16)
    held = [jnp.broadcast_to(jnp.where(group_row == g, 0.0, -BIG), (piece, HD)) for g in range(groups)]
    held = jnp.concatenate(held, axis=0).astype(jnp.bfloat16)
    for r in range(16):
        far_prefix[r * groups * piece : (r + 1) * groups * piece, :] = held
    factor = math.log2(math.e) / math.sqrt(HD)
    window = TILE + 2 * (HALO + 32)

    def attend(t):
        place = base + t * TILE + lax.broadcasted_iota(jnp.int32, (TILE, HD), 0)
        belongs = jnp.where((start_row <= place) & (place < end_row), 1.0, 0.0).astype(jnp.bfloat16)
        seen = slice(own + t * TILE - HALO - 32, own + t * TILE - HALO - 32 + window)
        made = []
        hidden_from = jnp.concatenate([far_prefix[...], far[seen, :]], axis=0)
        for h in range(heads):
            lanes = slice(h * HD, (h + 1) * HD)
            of_key, of_value = slice(2 * h * HD, (2 * h + 1) * HD), slice((2 * h + 1) * HD, (2 * h + 2) * HD)
            query = jnp.concatenate([q_all[t * TILE : (t + 1) * TILE, lanes], belongs], axis=1)
            key = jnp.concatenate([jnp.concatenate([prefix[:, of_key], near[seen, of_key]], axis=0), hidden_from], axis=1)
            score = lax.dot_general(query, key, (((1,), (1,)), ((), ())), preferred_element_type=jnp.float32)
            peak = jnp.max(score, axis=1, keepdims=True) * factor
            weight = jnp.exp2(score * factor - peak)
            mass = jnp.sum(weight, axis=1, keepdims=True)
            value = jnp.concatenate([prefix[:, of_value], near[seen, of_value]], axis=0)
            summed = jnp.dot(weight.astype(jnp.bfloat16), value, preferred_element_type=jnp.float32)
            made.append((summed / mass).astype(jnp.bfloat16))
        att_all[span(at.col * tokens + t * TILE, TILE), :] = jnp.concatenate(made, axis=1)

    attend(0)
    meet(met)
    outs[0].start()
    weights.start()
    attend(1)
    outs[1].start()
    outs[0].halves()
    weights.partner()
    outs[0].first(0)
    attend(2)
    outs[2].start()
    outs[0].first(1)
    weights.step(1)
    outs[1].halves()
    outs[1].first(0)
    weights.step(2)
    outs[0].second(0)
    outs[1].first(1)
    outs[2].halves()
    weights.step(3)
    outs[0].second(1)
    outs[2].first(0)
    outs[1].second(0)
    weights.step(4)
    outs[2].first(1)
    outs[1].second(1)
    weights.from_x()
    gate = contract_first(mod_ref[2], onehot)
    right = jnp.concatenate([w_out_all[j * features : (j + 1) * features, :] for j in range(16)], axis=1)

    def finish_tile(t):
        low, high = t * TILE, (t + 1) * TILE
        outs[t].from_core()
        left = jnp.concatenate([att_all[j * tokens + low : j * tokens + high, :] for j in range(16)], axis=1)
        made = lax.dot_general(right, left, (((1,), (1,)), ((), ())), preferred_element_type=jnp.float32)
        out_ref[:, low:high] = (hidden_ref[:, low:high].astype(jnp.float32) + gate[:, low:high] * made).astype(jnp.bfloat16)

    finish_tile(0)
    outs[2].second(0)
    outs[2].second(1)
    finish_tile(1)
    finish_tile(2)
    wire.drain()


def attend(req_len, req_group, mod, w_out_t, hidden, q, near, prefix):
    tokens, own = q.shape
    features = hidden.shape[0]
    vmem = pl.BlockSpec(memory_space=pltpu.VMEM)
    return pl.pallas_call(
        attend_kernel,
        out_shape=jax.ShapeDtypeStruct(hidden.shape, jnp.bfloat16),
        in_specs=[pl.BlockSpec(memory_space=pltpu.SMEM)] * 2 + [vmem] * 6,
        out_specs=vmem,
        scratch_shapes=[
            pltpu.VMEM((near.shape[0], HD), jnp.bfloat16),
            pltpu.VMEM((prefix.shape[0], HD), jnp.bfloat16),
            pltpu.VMEM((16 * tokens, own), jnp.bfloat16),
            pltpu.VMEM((16 * features, own), jnp.bfloat16),
            pltpu.SemaphoreType.DMA((96,)),
            pltpu.SemaphoreType.DMA((96,)),
        ],
        compiler_params=pltpu.CompilerParams(collective_id=1, has_side_effects=True, vmem_limit_bytes=VMEM_LIMIT),
        name="attend",
    )(req_len, req_group, mod, w_out_t, hidden, q, near, prefix)


def shards(hidden_in, modulation, w_qkv, w_out, prefix_cache, req_group, req_len, owner):
    tokens = hidden_in.shape[0]
    requests = req_len.shape[0]
    first = lax.axis_index("row") * tokens
    earlier = jnp.arange(requests)[:, None] > jnp.arange(requests)[None, :]
    starts = jnp.sum(jnp.where(earlier, req_len[None, :], 0), axis=1)
    ends = starts + req_len
    place = first + jnp.arange(tokens, dtype=jnp.int32)
    inside = (starts[:, None] <= place[None, :]) & (place[None, :] < ends[:, None])
    onehot_t = inside.astype(jnp.bfloat16)
    mod = jnp.transpose(modulation, (1, 0, 2))
    hidden_t = jnp.transpose(hidden_in)
    q, new_keys, new_values, near, prefix = project(
        owner, hidden_t, mod, onehot_t, w_qkv, prefix_cache[0]
    )
    hidden_out = attend(req_len, req_group, mod, jnp.transpose(w_out), hidden_t, q, near, prefix)
    return jnp.transpose(hidden_out), new_keys, new_values


def solution(mesh):
    return jax.shard_map(
        shards,
        mesh=mesh,
        in_specs=(
            P("row", "col"),
            P(None, None, "col"),
            P("row", "col"),
            P("row", "col"),
            P("row", None, "col"),
            P(),
            P(),
            P(),
        ),
        out_specs=(P("row", "col"), P("row", "col"), P("row", "col")),
        check_vma=False,
    )
```
